256 devices in a mesh: gx: 16 (over x_hi, z), gy: 16 (over x_lo, y, core).
Axes of the slice: x: 4 (x_hi: 2, x_lo: 2; x = x_hi * 2 + x_lo), y: 4, z: 8, core: 2. Of those that a mesh axis runs over, the one named last changes fastest.
Arguments:
- trial_stress: float32 [16, 2048, 2048], P(None, 'gx', 'gy'), may hold values from 1.5 to 3.5
- old_strain: float32 [16, 2048, 2048], P(None, 'gx', 'gy'), may hold values from 0 to 0.5
- yield_mask: int32 [16, 2048, 2048], P(None, 'gx', 'gy'), may hold values from 0 to 1
- newton_count: int32 [16, 2048, 2048], P(None, 'gx', 'gy'), may hold values from 3 to 6
- damage_threshold: float32 [16, 2048, 2048], P(None, 'gx', 'gy'), may hold values from 0.1 to 0.5
Outputs:
- plastic_strain: float32 [16, 2048, 2048], P(None, 'gx', 'gy')
- damage: float32 [16, 2048, 2048], P(None, 'gx', 'gy')
- nodal_force: float32 [2, 16, 2048, 2048], P(None, None, 'gx', 'gy')
The draws below stay inside these ranges and needn't reach their ends.
All inputs are finite; a program needn't handle non-finite values.
Results may differ from the reference program's by a relative error of at most 0.00002.
Values sent between devices are 32-bit elements; how exact they have to be, the bound alone decides.
A program may use at most 64 MiB of HBM per device.

```python
import math
import jax
import jax.numpy as jnp
from jax import lax

CZ = 16
NEWTON_MAX = 6
OUTER = 3
NX = 2048
NY = 2048


def draw_yield_mask(key, part):
    key_centre, key_coin = jax.random.split(key)
    centre = jax.random.randint(key_centre, (), 0, NX)
    row_ids = jnp.arange(NX, dtype=jnp.int32)
    distance = jnp.abs(row_ids - centre)
    distance = jnp.minimum(distance, NX - distance)
    inside = (distance * 16 < 3 * NX).astype(jnp.int32)
    coin_flip = jax.random.randint(key_coin, (CZ, NX, NY), 0, 2)
    return (coin_flip * inside[None, :, None]).astype(jnp.int32)


def plant(array, key, least, top_value):
    longest = array.shape.index(max(array.shape))
    spots = []
    for shift in (0, 1):
        where = [jax.random.randint(jax.random.fold_in(key, axis), (), 0, length) for axis, length in enumerate(array.shape)]
        where[longest] = (where[longest] + shift) % array.shape[longest]
        spots.append(tuple(where))
    return array.at[spots[0]].set(least).at[spots[1]].set(top_value)


def levels(rng, extent, cuts, least, largest):
    def one(dim, parts):
        steps = jax.random.uniform(jax.random.fold_in(jax.random.fold_in(rng, 6), dim), (parts,), jnp.float32, least / len(cuts), largest / len(cuts))
        return jnp.repeat(jnp.exp(steps), extent[dim] // parts).reshape((-1,) + (1,) * (len(extent) - dim - 1))

    loudness = one(*cuts[0])
    for cut in cuts[1:]:
        loudness = loudness * one(*cut)
    return loudness


def setup_inputs(seed: int = 0) -> dict:
    keys = jax.random.split(jax.random.key(seed), 6)
    trial_stress = jnp.clip(1.5 + 2.0 * jax.random.uniform(keys[0], (CZ, NX, NY), jnp.float32) ** levels(keys[0], (CZ, NX, NY), ((1, 16), (2, 16)), -0.2, 0.2), 1.5, 3.5)
    old_strain = jnp.clip(0.5 * jax.random.uniform(keys[1], (CZ, NX, NY), jnp.float32) ** levels(keys[1], (CZ, NX, NY), ((1, 16), (2, 16)), -0.2, 0.2), 0.0, 0.5)
    yield_mask = draw_yield_mask(jax.random.fold_in(keys[5], 71), 0)
    newton_count = plant(jax.random.randint(keys[3], (CZ, NX, NY), 3, NEWTON_MAX + 1), jax.random.fold_in(keys[3], 1), 3, NEWTON_MAX).astype(jnp.int32)
    damage_threshold = jnp.clip(0.1 + 0.4 * jax.random.uniform(keys[4], (CZ, NX, NY), jnp.float32) ** levels(keys[4], (CZ, NX, NY), ((1, 16), (2, 16)), -0.2, 0.2), 0.1, 0.5)
    return {"trial_stress": trial_stress, "old_strain": old_strain, "yield_mask": yield_mask, "newton_count": newton_count, "damage_threshold": damage_threshold}


gauss_taps = [math.exp(-((offset - 8) ** 2) / 32.0) for offset in range(17)]


def return_map(stress_in, strain_in, count_in, damage_in):
    increment = jnp.zeros_like(stress_in)
    soften = 1.0 - 0.5 * damage_in
    for sweep_no in range(1, NEWTON_MAX + 1):
        decay_term = jnp.exp(-4.0 * (strain_in + increment))
        residual = stress_in - increment - (1.0 + 0.5 * (1.0 - decay_term)) * soften
        update = increment + 0.4 * residual / (1.0 + 2.0 * decay_term)
        increment = jnp.where(count_in >= sweep_no, update, increment)
    return increment


def smooth_axis(source, axis_index):
    length = source.shape[axis_index]
    widths = [(0, 0)] * source.ndim
    widths[axis_index] = (8, 8)
    padded = jnp.pad(source, widths)
    summed = jnp.zeros_like(source)
    for offset in range(17):
        summed = summed + gauss_taps[offset] * lax.slice_in_dim(padded, offset, offset + length, axis=axis_index)
    return summed


def reference(trial_stress, old_strain, yield_mask, newton_count, damage_threshold):
    counts = yield_mask * newton_count
    weight_z = smooth_axis(jnp.ones((trial_stress.shape[0],), jnp.float32), 0)
    weight_x = smooth_axis(jnp.ones((trial_stress.shape[1],), jnp.float32), 0)
    weight_y = smooth_axis(jnp.ones((trial_stress.shape[2],), jnp.float32), 0)
    normal = weight_z[:, None, None] * weight_x[None, :, None] * weight_y[None, None, :]
    damage = jnp.zeros_like(trial_stress)
    for outer_no in range(OUTER):
        increment = return_map(trial_stress, old_strain, counts, damage)
        plastic_strain = old_strain + increment
        averaged = smooth_axis(smooth_axis(smooth_axis(plastic_strain, 1), 2), 0)
        nonlocal_strain = averaged / normal
        damage = 1.0 - jnp.exp(-jnp.maximum(nonlocal_strain - damage_threshold, 0.0) / 0.3)
    stress = (1.0 - damage) * (trial_stress - increment)
    padded = jnp.pad(stress, ((0, 0), (1, 0), (1, 0)))
    own_cell = padded[:, 1:, 1:]
    upper_cell = padded[:, :-1, 1:]
    left_cell = padded[:, 1:, :-1]
    corner_cell = padded[:, :-1, :-1]
    force_x = 0.5 * (upper_cell + corner_cell - own_cell - left_cell)
    force_y = 0.5 * (left_cell + corner_cell - own_cell - upper_cell)
    return plastic_strain, damage, jnp.stack([force_x, force_y])
```

```python
import functools
import math

import jax
import jax.numpy as jnp
import numpy as np
from jax import lax
from jax.experimental import pallas as pl
from jax.experimental.pallas import tpu as pltpu
from jax.sharding import PartitionSpec as P

NEWTON_MAX = 6
OUTER = 3
CZ = 16
B = 128
R = 8
ROWS = 16
BLOCKS = B // ROWS
LOG2E = 1.0 / math.log(2.0)
KAPPA = 4.0 * LOG2E
LOG5 = math.log2(5.0)
F32 = jnp.float32
BF16 = jnp.bfloat16
MESH = pl.DeviceIdType.MESH


def tap(t):
    t = np.asarray(t, np.float64)
    return np.where(np.abs(t) <= R, np.exp(-t * t / 32.0), 0.0)


def two(m):
    hi = np.asarray(m, np.float64).astype(BF16)
    lo = (m - hi.astype(np.float64)).astype(BF16)
    return hi, lo


def axis_norm(first, last, n):
    at = np.arange(n)
    norm = np.zeros(n)
    for off in range(-R, R + 1):
        to = at + off
        inside = np.ones(n, bool)
        if first:
            inside &= to >= 0
        if last:
            inside &= to < n
        norm += np.where(inside, tap(off), 0.0)
    return norm


def axis_matrix(first, last):
    out = np.arange(B)[:, None]
    col = np.arange(B + 2 * R)[None, :] - R
    return tap(out - col) / axis_norm(first, last, B)[:, None]


def depth_matrix():
    at = np.arange(CZ)
    return tap(at[:, None] - at[None, :]) / axis_norm(True, True, CZ)[:, None]


def tables():
    wy, wx, ae = [], [], []
    for first, last in ((True, False), (False, False), (False, True)):
        ext = axis_matrix(first, last)
        own = ext[:, R : R + B]
        hi, lo = two(own.T)
        wy.append(np.block([[hi, lo], [hi, lo]]))
        hi, lo = two(own)
        wx.append(np.block([[hi, hi], [lo, lo]]))
        wide = np.zeros((B, 2 * B))
        wide[:, : B + 2 * R] = ext
        ae.append(np.concatenate(two(wide), axis=0))
    az = depth_matrix()
    full = np.exp(-(np.arange(-R, R + 1) ** 2) / 32.0).sum()
    by = np.zeros((2 * B, 2 * B))
    bx = np.zeros((2 * B, 2 * B))
    for z in range(CZ):
        for j in range(R):
            lane = 16 * (z % 8) + 8 * (z // 8) + j
            for zo in range(CZ):
                base = 128 * (zo // 8) + 16 * (zo % 8)
                for r in range(R):
                    by[lane, base + 8 + r] = az[zo, z] * tap(r - (j - 8)) / full
                    by[B + lane, base + r] = az[zo, z] * tap(r - 8 - j) / full
                    bx[8 * zo + r, 8 * z + j] = az[zo, z] * tap(r - (j - 8)) / full
                    bx[B + 8 * zo + r, B + 8 * z + j] = az[zo, z] * tap(r - 8 - j) / full
    return (
        np.stack(wy),
        np.stack(wx),
        np.stack(ae),
        np.stack(two(by)),
        np.concatenate(two(bx), axis=0),
    )


def split(v):
    hi = v.astype(BF16)
    return hi, (v - hi.astype(F32)).astype(BF16)


def dot(a, b):
    return jnp.dot(a, b, preferred_element_type=F32)


def recip(v):
    r = pltpu.reciprocal(v, approx=True)
    return r * (2.0 - v * r)


def newton(start, goal, beta, count):
    y = start
    for s in range(1, NEWTON_MAX + 1):
        part = y * recip(jnp.exp2(y - goal) + 2.5)
        moved = (y - beta) - part
        y = moved if s <= 3 else jnp.where(count >= s, moved, y)
    return (goal - y) * (1.0 / KAPPA) + LOG5 / KAPPA


def depth_halves():
    az = depth_matrix()
    return 0.5 * (az[:8, :8] + az[:8, :7:-1]), 0.5 * (az[:8, :8] - az[:8, :7:-1])


def smooth_depth(planes):
    even, odd = depth_halves()
    add = [planes[z] + planes[CZ - 1 - z] for z in range(8)]
    sub = [planes[z] - planes[CZ - 1 - z] for z in range(8)]
    out = [None] * CZ
    for z in range(8):
        e = float(even[z, 0]) * add[0]
        o = float(odd[z, 0]) * sub[0]
        for i in range(1, 8):
            e = e + float(even[z, i]) * add[i]
            o = o + float(odd[z, i]) * sub[i]
        out[z] = e + o
        out[CZ - 1 - z] = e - o
    return out


KERNEL_VMEM = 30 << 20
FORCE_VMEM = 12 << 20
CHUNKS = ((0, 16), (112, 16), (16, 48), (64, 48))


def kernel(
    nx, ny,
    t_h, old_h, mask_h, cnt_h, thr_h, wy_h, wx_h, ae_h, by_h, bx_h,
    p_o, d_o, se, frec,
    t_v, old_v, mask_v, cnt_v, thr_v, g_v, p_s, zhl, t2, nl, hout, yhi, ylo, pack, hrec, xrec,
    wy, wx, ae, by, bx, fpack,
    in_sem, w_sem, send, recv,
):
    gx = lax.axis_index("gx")
    gy = lax.axis_index("gy")
    p_v = [p_s.at[0], p_s.at[1], p_o]
    up, dn, lf, rt = gx > 0, gx < nx - 1, gy > 0, gy < ny - 1

    def variant(i, n):
        return jnp.where(i == 0, 0, jnp.where(i == n - 1, 2, 1))

    ins = ((t_h, t_v), (old_h, old_v), (mask_h, mask_v), (cnt_h, cnt_v), (thr_h, thr_v))
    loads = []
    for c, (r0, n) in enumerate(CHUNKS):
        for a, (src, dst) in enumerate(ins[:4]):
            copy = pltpu.make_async_copy(src.at[:, r0 : r0 + n, :], dst.at[:, r0 : r0 + n, :], in_sem.at[c, a])
            copy.start()
            loads.append(copy)
    weights = [
        pltpu.make_async_copy(wy_h.at[variant(gy, ny)], wy, w_sem.at[0]),
        pltpu.make_async_copy(wx_h.at[variant(gx, nx)], wx, w_sem.at[1]),
        pltpu.make_async_copy(ae_h.at[variant(gx, nx)], ae, w_sem.at[2]),
        pltpu.make_async_copy(by_h, by, w_sem.at[3]),
        pltpu.make_async_copy(bx_h, bx, w_sem.at[4]),
        pltpu.make_async_copy(thr_h, thr_v, w_sem.at[5]),
    ]
    for copy in weights:
        copy.start()

    barrier = pltpu.get_barrier_semaphore()
    for dx in (-1, 0, 1):
        for dy in (-1, 0, 1):
            if dx == 0 and dy == 0:
                continue
            here = [c for c, on in ((up, dx < 0), (dn, dx > 0), (lf, dy < 0), (rt, dy > 0)) if on]

            @pl.when(functools.reduce(jnp.logical_and, here))
            def _(dx=dx, dy=dy):
                pl.semaphore_signal(barrier, inc=1, device_id=(gx + dx, gy + dy), device_id_type=MESH)

    one = jnp.int32(1)
    zero = jnp.int32(0)
    across = jnp.where(up, one, zero) + jnp.where(dn, one, zero) + 1
    along = jnp.where(lf, one, zero) + jnp.where(rt, one, zero) + 1
    pl.semaphore_wait(barrier, across * along - 1)

    @pl.when(jnp.logical_not(up))
    def _():
        for k in range(OUTER):
            xrec[k, 0] = jnp.zeros((CZ, R, B), F32)
            hrec[k, :, 0:R, :] = jnp.zeros((2, R, B), F32)
        se[:, 0:R, :] = jnp.zeros((CZ, R, B), F32)
        frec[0:R, :] = jnp.zeros((R, B), F32)

    @pl.when(jnp.logical_not(dn))
    def _():
        for k in range(OUTER):
            xrec[k, 1] = jnp.zeros((CZ, R, B), F32)
            hrec[k, :, R + B :, :] = jnp.zeros((2, R, B), F32)

    @pl.when(jnp.logical_not(lf))
    def _():
        for k in range(OUTER):
            hrec[k, 0] = jnp.zeros((B + 2 * R, B), F32)
        frec[...] = jnp.zeros((B + R, B), F32)

    @pl.when(jnp.logical_not(rt))
    def _():
        for k in range(OUTER):
            hrec[k, 1] = jnp.zeros((B + 2 * R, B), F32)

    yhi[...] = jnp.zeros_like(yhi)
    ylo[...] = jnp.zeros_like(ylo)

    lane = lax.broadcasted_iota(jnp.int32, (ROWS, B), 1)
    slot = lane // 16
    low = (lane % 16) < 8
    rim = jnp.logical_or(lane < R, lane >= B - R)

    def rdma(k, i, src, dst, dx, dy):
        ix = jnp.clip(gx + dx, 0, nx - 1)
        iy = jnp.clip(gy + dy, 0, ny - 1)
        return pltpu.make_async_remote_copy(
            src_ref=src, dst_ref=dst, send_sem=send.at[k, i], recv_sem=recv.at[k, i],
            device_id=(ix, iy), device_id_type=MESH,
        )

    def faces(k):
        both = jnp.logical_and
        top, bottom = slice(0, R), slice(B - R, B)
        after = slice(R + B, 2 * R + B)
        return [
            (up, dn, rdma(k, 0, p_v[k].at[:, top, :], xrec.at[k, 1], -1, 0)),
            (dn, up, rdma(k, 1, p_v[k].at[:, bottom, :], xrec.at[k, 0], 1, 0)),
            (both(dn, rt), both(up, lf), rdma(k, 2, pack.at[k, 1, bottom], hrec.at[k, 0, top], 1, 1)),
            (both(up, rt), both(dn, lf), rdma(k, 3, pack.at[k, 1, top], hrec.at[k, 0, after], -1, 1)),
            (both(dn, lf), both(up, rt), rdma(k, 4, pack.at[k, 0, bottom], hrec.at[k, 1, top], 1, -1)),
            (both(up, lf), both(dn, rt), rdma(k, 5, pack.at[k, 0, top], hrec.at[k, 1, after], -1, -1)),
        ]

    def sides(k, c):
        r0, n = CHUNKS[c]
        here, there = slice(r0, r0 + n), slice(R + r0, R + r0 + n)
        return [
            (rt, lf, rdma(k, 6 + 2 * c, pack.at[k, 1, here], hrec.at[k, 0, there], 0, 1)),
            (lf, rt, rdma(k, 7 + 2 * c, pack.at[k, 0, here], hrec.at[k, 1, there], 0, -1)),
        ]

    def start(copies):
        for sends, _, copy in copies:
            pl.when(sends)(copy.start)

    def finish(copies):
        for sends, gets, copy in copies:
            pl.when(gets)(copy.wait_recv)
            pl.when(sends)(copy.wait_send)

    def block_of(i):
        return jnp.where(i == 0, 0, jnp.where(i == 1, BLOCKS - 1, i - 1))

    def rows_of(i):
        return pl.ds(pl.multiple_of(block_of(i) * ROWS, ROWS), ROWS)

    def halo_add(z, at):
        h, zz = z // 8, z % 8
        part = pltpu.roll(hout[at, 128 * h : 128 * h + 128], (120 - 16 * zz) % 128, 1)
        return nl[z, at, :] + jnp.where(rim, part, 0.0)

    def damage_left(z, at):
        over = jnp.maximum(halo_add(z, at) - thr_v[z, at, :], 0.0)
        return jnp.exp2(over * (-LOG2E / 0.3))

    def update(k, i):
        at = rows_of(i)
        for z in range(CZ):
            if k == 0:
                t, old = t_v[z, at, :], old_v[z, at, :]
                count = mask_v[z, at, :] * cnt_v[z, at, :]
                cnt_v[z, at, :] = count
                g0 = KAPPA * (t + old) - LOG5
                y0 = KAPPA * t
                g_v[z, at, :] = g0
                t_v[z, at, :] = y0
                beta = 0.1 * KAPPA
                p = newton(y0 - 17.5 * beta, g0 - 17.5 * beta, beta, count)
            else:
                old = old_v[z, at, :]
                count = cnt_v[z, at, :]
                beta = (0.05 * KAPPA) * damage_left(z, at) + 0.05 * KAPPA
                reach = 17.5 * beta
                p = newton(t_v[z, at, :] - reach, g_v[z, at, :] - reach, beta, count)
            p_v[k][z, at, :] = jnp.where(count > 0, p, old)
        halves = []
        for h in range(2):
            acc = None
            for zz in range(8):
                turned = pltpu.roll(p_v[k][8 * h + zz, at, :], (16 * zz + 8) % 128, 1)
                acc = turned if acc is None else jnp.where(slot == zz, turned, acc)
            halves.append(acc)
        a, b = halves
        pack[k, 1, at, :] = jnp.where(low, a, pltpu.roll(b, 8, 1))
        pack[k, 0, at, :] = jnp.where(low, pltpu.roll(a, 120, 1), b)
        for r in range(0, ROWS, 8):
            at8 = pl.ds(pl.multiple_of(block_of(i) * ROWS + r, 8), 8)
            for z, plane in enumerate(smooth_depth([p_v[k][z, at8, :] for z in range(CZ)])):
                zhl[z, r : r + 8, :] = plane
        hi, lo = split(zhl[...].reshape(CZ * ROWS, B))
        t = dot(jnp.concatenate([hi, lo], axis=1), wy[...])
        hi, lo = split(t[:, :B] + t[:, B:])
        below = pl.ds(pl.multiple_of(block_of(i) * ROWS + B, ROWS), ROWS)
        for z in range(CZ):
            half, rows = pl.ds(128 * (z % 2), 128), slice(ROWS * z, ROWS * z + ROWS)
            t2[z // 2, at, half] = hi[rows]
            t2[z // 2, below, half] = lo[rows]

    def sweep_all(k):
        def body(i, carry):
            if k == 0:
                for c in range(4):
                    @pl.when(i == (0, 1, 2, 5)[c])
                    def _(c=c):
                        for copy in loads[4 * c : 4 * c + 4]:
                            copy.wait()
                @pl.when(i == 0)
                def _():
                    for copy in weights:
                        copy.wait()

            update(k, i)

            @pl.when(i == 1)
            def _():
                start(faces(k))
                start(sides(k, 0))
                start(sides(k, 1))

            @pl.when(i == 4)
            def _():
                start(sides(k, 2))

            return carry

        lax.fori_loop(0, BLOCKS, body, 0)
        start(sides(k, 3))

    def own_rows():
        def body(i, carry):
            o = dot(wx[...], t2[i])
            o = o[:B] + o[B:]
            nl[2 * i] = o[:, :B]
            nl[2 * i + 1] = o[:, B:]
            return carry

        lax.fori_loop(0, CZ // 2, body, 0)

    def halos(k):
        finish(faces(k))
        for c in range(4):
            finish(sides(k, c))
        hi, lo = split(jnp.concatenate([hrec[k, 0], hrec[k, 1]], axis=1))
        yh = dot(hi, by[0]) + dot(lo, by[0]) + dot(hi, by[1])
        hi, lo = split(yh)
        yhi[0 : B + 2 * R, :] = hi
        ylo[0 : B + 2 * R, :] = lo
        both = dot(ae[...], yhi[...])
        hout[...] = both[:B] + both[B:] + dot(ae[:B, :], ylo[...])
        hi, lo = split(xrec[k].reshape(2 * B, B))
        g = dot(jnp.concatenate([hi, lo], axis=1), wy[...])
        hi, lo = split(g[:, :B] + g[:, B:])
        o = dot(bx[...], jnp.concatenate([hi, lo], axis=1))
        o = o[: 2 * B, :B] + o[: 2 * B, B:] + o[2 * B :, :B]
        o = o.reshape(2, CZ, R, B)
        nl[:, 0:R, :] += o[0]
        nl[:, B - R :, :] += o[1]

    for k in range(OUTER):
        sweep_all(k)
        own_rows()
        halos(k)

    def last(i, carry):
        at = rows_of(i)
        acc = jnp.zeros((ROWS, B), F32)
        inside = pl.ds(pl.multiple_of(block_of(i) * ROWS + R, R), ROWS)
        for z in range(CZ):
            left = damage_left(z, at)
            d_o[z, at, :] = 1.0 - left
            stress = left * ((g_v[z, at, :] + LOG5) * (1.0 / KAPPA) - p_o[z, at, :])
            se[z, inside, :] = stress
            acc = jnp.where(lane == z, pltpu.roll(stress, (z + 1) % 128, 1), acc)
        fpack[at, :] = acc
        return carry

    lax.fori_loop(0, BLOCKS, last, 0)
    both = jnp.logical_and
    ends = [
        (rt, lf, rdma(OUTER, 0, fpack, frec.at[R:, :], 0, 1)),
        (dn, up, rdma(OUTER, 1, se.at[:, B + R - 1 : B + R, :], se.at[:, R - 1 : R, :], 1, 0)),
        (both(dn, rt), both(up, lf), rdma(OUTER, 2, fpack.at[B - R :, :], frec.at[:R, :], 1, 1)),
    ]
    start(ends)
    finish(ends)


def forces(se, frec, p_v, d_v, p_h, d_h, f_h, f_v, sem):
    copies = [pltpu.make_async_copy(p_v, p_h, sem.at[0]), pltpu.make_async_copy(d_v, d_h, sem.at[1])]
    for copy in copies:
        copy.start()
    lane8 = lax.broadcasted_iota(jnp.int32, (R, B), 1)
    row8 = lax.broadcasted_iota(jnp.int32, (R, B), 0)

    for z in range(CZ):
        above = left = None
        for i in range(B // R + 1):
            at8 = slice(R * i, R * i + R)
            s = se[z, at8, :]
            col = frec[at8, :]
            if z:
                col = pltpu.roll(col, 128 - z, 1)
            l = jnp.where(lane8 == 0, col, pltpu.roll(s, 1, 1))
            if i:
                s_up = pltpu.roll(jnp.where(row8 == R - 1, above, s), 1, 0)
                l_up = pltpu.roll(jnp.where(row8 == R - 1, left, l), 1, 0)
                a = 0.5 * (l_up - s)
                b = 0.5 * (s_up - l)
                f_v[0, z, R * i - R : R * i, :] = a + b
                f_v[1, z, R * i - R : R * i, :] = a - b
            above, left = s, l
        for c in range(2):
            copies.append(pltpu.make_async_copy(f_v.at[c, z], f_h.at[c, z], sem.at[2 + 2 * z + c]))
            copies[-1].start()
    for copy in copies:
        copy.wait()


def solution(mesh):
    nx, ny = mesh.shape["gx"], mesh.shape["gy"]
    consts = tables()
    hbm = pl.BlockSpec(memory_space=pltpu.MemorySpace.HBM)
    vmem = pl.BlockSpec(memory_space=pltpu.MemorySpace.VMEM)
    block = jax.ShapeDtypeStruct((CZ, B, B), F32)
    scratch = [
        pltpu.VMEM((CZ, B, B), F32),
        pltpu.VMEM((CZ, B, B), F32),
        pltpu.VMEM((CZ, B, B), jnp.int32),
        pltpu.VMEM((CZ, B, B), jnp.int32),
        pltpu.VMEM((CZ, B, B), F32),
        pltpu.VMEM((CZ, B, B), F32),
        pltpu.VMEM((OUTER - 1, CZ, B, B), F32),
        pltpu.VMEM((CZ, ROWS, B), F32),
        pltpu.VMEM((CZ // 2, 2 * B, 2 * B), BF16),
        pltpu.VMEM((CZ, B, B), F32),
        pltpu.VMEM((B, 2 * B), F32),
        pltpu.VMEM((2 * B, 2 * B), BF16),
        pltpu.VMEM((2 * B, 2 * B), BF16),
        pltpu.VMEM((OUTER, 2, B, B), F32),
        pltpu.VMEM((OUTER, 2, B + 2 * R, B), F32),
        pltpu.VMEM((OUTER, 2, CZ, R, B), F32),
        pltpu.VMEM((2 * B, 2 * B), BF16),
        pltpu.VMEM((2 * B, 2 * B), BF16),
        pltpu.VMEM((2 * B, 2 * B), BF16),
        pltpu.VMEM((2, 2 * B, 2 * B), BF16),
        pltpu.VMEM((4 * B, 2 * B), BF16),
        pltpu.VMEM((B, B), F32),
        pltpu.SemaphoreType.DMA((4, 4)),
        pltpu.SemaphoreType.DMA((6,)),
        pltpu.SemaphoreType.DMA((OUTER + 1, 14)),
        pltpu.SemaphoreType.DMA((OUTER + 1, 14)),
    ]

    def local(*args):
        p, d, stress, column = pl.pallas_call(
            functools.partial(kernel, nx, ny),
            out_shape=(
                block,
                block,
                jax.ShapeDtypeStruct((CZ, B + R, B), F32),
                jax.ShapeDtypeStruct((B + R, B), F32),
            ),
            in_specs=[hbm] * 10,
            out_specs=[vmem] * 4,
            scratch_shapes=scratch,
            compiler_params=pltpu.CompilerParams(
                collective_id=0, has_side_effects=True, vmem_limit_bytes=KERNEL_VMEM
            ),
        )(*[pltpu.with_memory_space_constraint(a, pltpu.MemorySpace.HBM) for a in (*args, *[jnp.asarray(c) for c in consts])])
        return pl.pallas_call(
            forces,
            out_shape=(block, block, jax.ShapeDtypeStruct((2, CZ, B, B), F32)),
            in_specs=[vmem] * 4,
            out_specs=[hbm] * 3,
            scratch_shapes=[pltpu.VMEM((2, CZ, B, B), F32), pltpu.SemaphoreType.DMA((2 + 2 * CZ,))],
            compiler_params=pltpu.CompilerParams(vmem_limit_bytes=FORCE_VMEM),
        )(stress, column, p, d)

    placed = P(None, "gx", "gy")
    return jax.shard_map(
        local,
        mesh=mesh,
        in_specs=(placed,) * 5,
        out_specs=(placed, placed, P(None, None, "gx", "gy")),
        check_vma=False,
    )
```

```python
import functools
import math

import jax
import jax.numpy as jnp
import numpy as np
from jax import lax
from jax.experimental import pallas as pl
from jax.experimental.pallas import tpu as pltpu
from jax.sharding import PartitionSpec as P

NEWTON_MAX = 6
OUTER = 3
CZ = 16
B = 128
R = 8
ROWS = 16
BLOCKS = B // ROWS
LOG2E = 1.0 / math.log(2.0)
SHIFT = 0.5 * math.log(2.0)
F32 = jnp.float32
BF16 = jnp.bfloat16
MESH = pl.DeviceIdType.MESH


def tap(t):
    t = np.asarray(t, np.float64)
    return np.where(np.abs(t) <= R, np.exp(-t * t / 32.0), 0.0)


def two(m):
    hi = np.asarray(m, np.float64).astype(BF16)
    lo = (m - hi.astype(np.float64)).astype(BF16)
    return hi, lo


def axis_norm(first, last, n):
    at = np.arange(n)
    norm = np.zeros(n)
    for off in range(-R, R + 1):
        to = at + off
        inside = np.ones(n, bool)
        if first:
            inside &= to >= 0
        if last:
            inside &= to < n
        norm += np.where(inside, tap(off), 0.0)
    return norm


def axis_matrix(first, last):
    out = np.arange(B)[:, None]
    col = np.arange(B + 2 * R)[None, :] - R
    return tap(out - col) / axis_norm(first, last, B)[:, None]


def depth_matrix():
    at = np.arange(CZ)
    return tap(at[:, None] - at[None, :]) / axis_norm(True, True, CZ)[:, None]


def tables():
    wy, wx, ae = [], [], []
    for first, last in ((True, False), (False, False), (False, True)):
        ext = axis_matrix(first, last)
        own = ext[:, R : R + B]
        hi, lo = two(own.T)
        wy.append(np.block([[hi, lo], [hi, lo]]))
        hi, lo = two(own)
        wx.append(np.block([[hi, hi], [lo, lo]]))
        wide = np.zeros((B, 2 * B))
        wide[:, : B + 2 * R] = ext
        ae.append(np.concatenate(two(wide), axis=0))
    az = depth_matrix()
    full = np.exp(-(np.arange(-R, R + 1) ** 2) / 32.0).sum()
    by = np.zeros((2 * B, 2 * B))
    bx = np.zeros((2 * B, 2 * B))
    for z in range(CZ):
        for j in range(R):
            lane = 16 * (z % 8) + 8 * (z // 8) + j
            for zo in range(CZ):
                base = 128 * (zo // 8) + 16 * (zo % 8)
                for r in range(R):
                    by[lane, base + 8 + r] = az[zo, z] * tap(r - (j - 8)) / full
                    by[B + lane, base + r] = az[zo, z] * tap(r - 8 - j) / full
                    bx[8 * zo + r, 8 * z + j] = az[zo, z] * tap(r - (j - 8)) / full
                    bx[B + 8 * zo + r, B + 8 * z + j] = az[zo, z] * tap(r - 8 - j) / full
    return (
        np.stack(wy),
        np.stack(wx),
        np.stack(ae),
        np.stack(two(by)),
        np.concatenate(two(bx), axis=0),
    )


def split(v):
    hi = v.astype(BF16)
    return hi, (v - hi.astype(F32)).astype(BF16)


def dot(a, b):
    return jnp.dot(a, b, preferred_element_type=F32)


def newton(start, goal, beta, count):
    y = start
    for s in range(1, NEWTON_MAX + 1):
        moved = y * (0.8 - 0.2 * jnp.tanh(goal - y)) - beta
        y = moved if s <= 3 else jnp.where(count >= s, moved, y)
    return 0.5 * (goal - y) + 0.5 * SHIFT


def depth_halves():
    az = depth_matrix()
    return 0.5 * (az[:8, :8] + az[:8, :7:-1]), 0.5 * (az[:8, :8] - az[:8, :7:-1])


def smooth_depth(planes):
    even, odd = depth_halves()
    add = [planes[z] + planes[CZ - 1 - z] for z in range(8)]
    sub = [planes[z] - planes[CZ - 1 - z] for z in range(8)]
    out = [None] * CZ
    for z in range(8):
        e = float(even[z, 0]) * add[0]
        o = float(odd[z, 0]) * sub[0]
        for i in range(1, 8):
            e = e + float(even[z, i]) * add[i]
            o = o + float(odd[z, i]) * sub[i]
        out[z] = e + o
        out[CZ - 1 - z] = e - o
    return out


KERNEL_VMEM = 30 << 20
FORCE_VMEM = 12 << 20
CHUNKS = ((0, 8), (120, 8), (8, 48), (56, 64))
SIDES = ((0, 56), (56, 48), (104, 24))


def kernel(
    nx, ny,
    t_h, old_h, mask_h, cnt_h, thr_h, wy_h, wx_h, ae_h, by_h, bx_h,
    p_o, d_o, f_o, se, frec,
    t_v, old_v, mask_v, cnt_v, thr_v, g_v, p_s, zhl, t2, nl, hout, yhi, ylo, pack, hrec, xrec,
    wy, wx, ae, by, bx, fpack,
    in_sem, w_sem, send, recv,
):
    gx = lax.axis_index("gx")
    gy = lax.axis_index("gy")
    p_v = [p_s.at[0], p_s.at[1], p_o]
    up, dn, lf, rt = gx > 0, gx < nx - 1, gy > 0, gy < ny - 1

    def variant(i, n):
        return jnp.where(i == 0, 0, jnp.where(i == n - 1, 2, 1))

    ins = ((t_h, t_v), (old_h, old_v), (mask_h, mask_v), (cnt_h, cnt_v), (thr_h, thr_v))
    loads = []
    for c, (r0, n) in enumerate(CHUNKS):
        for a, (src, dst) in enumerate(ins[:4]):
            copy = pltpu.make_async_copy(src.at[:, r0 : r0 + n, :], dst.at[:, r0 : r0 + n, :], in_sem.at[c, a])
            copy.start()
            loads.append(copy)
    weights = [
        pltpu.make_async_copy(wy_h.at[variant(gy, ny)], wy, w_sem.at[0]),
        pltpu.make_async_copy(wx_h.at[variant(gx, nx)], wx, w_sem.at[1]),
        pltpu.make_async_copy(ae_h.at[variant(gx, nx)], ae, w_sem.at[2]),
        pltpu.make_async_copy(by_h, by, w_sem.at[3]),
        pltpu.make_async_copy(bx_h, bx, w_sem.at[4]),
        pltpu.make_async_copy(thr_h, thr_v, w_sem.at[5]),
    ]
    for copy in weights:
        copy.start()

    barrier = pltpu.get_barrier_semaphore()
    for dx in (-1, 0, 1):
        for dy in (-1, 0, 1):
            if dx == 0 and dy == 0:
                continue
            here = [c for c, on in ((up, dx < 0), (dn, dx > 0), (lf, dy < 0), (rt, dy > 0)) if on]

            @pl.when(functools.reduce(jnp.logical_and, here))
            def _(dx=dx, dy=dy):
                pl.semaphore_signal(barrier, inc=1, device_id=(gx + dx, gy + dy), device_id_type=MESH)

    one = jnp.int32(1)
    zero = jnp.int32(0)
    across = jnp.where(up, one, zero) + jnp.where(dn, one, zero) + 1
    along = jnp.where(lf, one, zero) + jnp.where(rt, one, zero) + 1

    def enter():
        pl.semaphore_wait(barrier, across * along - 1)

    @pl.when(jnp.logical_not(up))
    def _():
        for k in range(OUTER):
            xrec[k, 0] = jnp.zeros((CZ, R, B), F32)
            hrec[k, :, 0:R, :] = jnp.zeros((2, R, B), F32)
        se[:, 0:R, :] = jnp.zeros((CZ, R, B), F32)
        frec[0:R, :] = jnp.zeros((R, B), F32)

    @pl.when(jnp.logical_not(dn))
    def _():
        for k in range(OUTER):
            xrec[k, 1] = jnp.zeros((CZ, R, B), F32)
            hrec[k, :, R + B :, :] = jnp.zeros((2, R, B), F32)

    @pl.when(jnp.logical_not(lf))
    def _():
        for k in range(OUTER):
            hrec[k, 0] = jnp.zeros((B + 2 * R, B), F32)
        frec[...] = jnp.zeros((B + R, B), F32)

    @pl.when(jnp.logical_not(rt))
    def _():
        for k in range(OUTER):
            hrec[k, 1] = jnp.zeros((B + 2 * R, B), F32)

    yhi[...] = jnp.zeros_like(yhi)
    ylo[...] = jnp.zeros_like(ylo)

    lane = lax.broadcasted_iota(jnp.int32, (R, B), 1)
    slot = lane // 16
    low = (lane % 16) < 8
    rim = jnp.logical_or(lane < R, lane >= B - R)

    def rdma(k, i, src, dst, dx, dy):
        ix = jnp.clip(gx + dx, 0, nx - 1)
        iy = jnp.clip(gy + dy, 0, ny - 1)
        return pltpu.make_async_remote_copy(
            src_ref=src, dst_ref=dst, send_sem=send.at[k, i], recv_sem=recv.at[k, i],
            device_id=(ix, iy), device_id_type=MESH,
        )

    def faces(k):
        both = jnp.logical_and
        top, bottom = slice(0, R), slice(B - R, B)
        after = slice(R + B, 2 * R + B)
        return [
            (up, dn, rdma(k, 0, p_v[k].at[:, top, :], xrec.at[k, 1], -1, 0)),
            (dn, up, rdma(k, 1, p_v[k].at[:, bottom, :], xrec.at[k, 0], 1, 0)),
            (both(dn, rt), both(up, lf), rdma(k, 2, pack.at[k, 1, bottom], hrec.at[k, 0, top], 1, 1)),
            (both(up, rt), both(dn, lf), rdma(k, 3, pack.at[k, 1, top], hrec.at[k, 0, after], -1, 1)),
            (both(dn, lf), both(up, rt), rdma(k, 4, pack.at[k, 0, bottom], hrec.at[k, 1, top], 1, -1)),
            (both(up, lf), both(dn, rt), rdma(k, 5, pack.at[k, 0, top], hrec.at[k, 1, after], -1, -1)),
        ]

    def sides(k, c):
        r0, n = SIDES[c]
        here, there = slice(r0, r0 + n), slice(R + r0, R + r0 + n)
        return [
            (rt, lf, rdma(k, 6 + 2 * c, pack.at[k, 1, here], hrec.at[k, 0, there], 0, 1)),
            (lf, rt, rdma(k, 7 + 2 * c, pack.at[k, 0, here], hrec.at[k, 1, there], 0, -1)),
        ]

    def start(copies):
        for sends, _, copy in copies:
            pl.when(sends)(copy.start)

    def finish(copies):
        for sends, gets, copy in copies:
            pl.when(gets)(copy.wait_recv)
            pl.when(sends)(copy.wait_send)

    def rows_of(i):
        first = jnp.where(i == 0, 0, ROWS * i - R)
        second = jnp.where(i == 0, B - R, ROWS * i)
        return [pl.ds(pl.multiple_of(first, R), R), pl.ds(pl.multiple_of(second, R), R)]

    def packed(read):
        halves = []
        for h in range(2):
            acc = None
            for zz in range(8):
                turned = pltpu.roll(read(8 * h + zz), (16 * zz + 8) % 128, 1)
                acc = turned if acc is None else jnp.where(slot == zz, turned, acc)
            halves.append(acc)
        return interleave(*halves)

    def interleave(a, b):
        return jnp.where(low, pltpu.roll(a, 120, 1), b), jnp.where(low, a, pltpu.roll(b, 8, 1))

    def halo_add(z, at):
        h, zz = z // 8, z % 8
        part = pltpu.roll(hout[at, 128 * h : 128 * h + 128], (120 - 16 * zz) % 128, 1)
        return nl[z, at, :] + jnp.where(rim, part, 0.0)

    def damage_left(z, at):
        return decay(halo_add(z, at), thr_v[z, at, :])

    def solve(start, goal, old, count, left):
        beta = 0.2 if left is None else 0.1 * left + 0.1
        reach = 17.5 * beta
        return jnp.where(count > 0, newton(start - reach, goal - reach, beta, count), old)

    def decay(average, threshold):
        return jnp.exp2(jnp.maximum(average - threshold, 0.0) * (-LOG2E / 0.3))

    def update(k, i):
        for at in rows_of(i):
            for z in range(CZ):
                if k == 0:
                    t, old = t_v[z, at, :], old_v[z, at, :]
                    count = mask_v[z, at, :] * cnt_v[z, at, :]
                    cnt_v[z, at, :] = count
                    goal = 2.0 * (t + old) - SHIFT
                    start = 2.0 * t
                    g_v[z, at, :] = goal
                    t_v[z, at, :] = start
                    left = None
                else:
                    start, goal, old, count = t_v[z, at, :], g_v[z, at, :], old_v[z, at, :], cnt_v[z, at, :]
                    left = damage_left(z, at)
                p_v[k][z, at, :] = solve(start, goal, old, count, left)
            pack[k, 0, at, :], pack[k, 1, at, :] = packed(lambda z: p_v[k][z, at, :])

    def own_part(k):
        def depth(i, carry):
            at8 = pl.ds(pl.multiple_of(i * R, R), R)
            for z, plane in enumerate(smooth_depth([p_v[k][z, at8, :] for z in range(CZ)])):
                zhl[z, at8, :] = plane
            return carry

        lax.fori_loop(0, B // R, depth, 0)
        for b in range(BLOCKS):
            hi, lo = split(zhl[:, ROWS * b : ROWS * b + ROWS, :].reshape(CZ * ROWS, B))
            t = dot(jnp.concatenate([hi, lo], axis=1), wy[...])
            hi, lo = split(t[:, :B] + t[:, B:])
            for z in range(CZ):
                half, rows = slice(128 * (z % 2), 128 * (z % 2) + 128), slice(ROWS * z, ROWS * z + ROWS)
                t2[z // 2, ROWS * b : ROWS * b + ROWS, half] = hi[rows]
                t2[z // 2, B + ROWS * b : B + ROWS * b + ROWS, half] = lo[rows]
        for i in range(CZ // 2):
            o = dot(wx[...], t2[i])
            o = o[:B] + o[B:]
            nl[2 * i] = o[:, :B]
            nl[2 * i + 1] = o[:, B:]

    def sweep(k, lo, hi):
        def body(i, carry):
            update(k, i)
            return carry

        lax.fori_loop(lo, hi, body, 0)

    def arrived(c):
        for copy in loads[4 * c : 4 * c + 4]:
            copy.wait()

    def sweep_all(k):
        if k == 0:
            arrived(0)
            arrived(1)
        sweep(k, 0, 1)
        if k == 0:
            enter()
        start(faces(k))
        if k == 0:
            arrived(2)
        sweep(k, 1, 4)
        start(sides(k, 0))
        if k == 0:
            arrived(3)
            for copy in weights:
                copy.wait()
        sweep(k, 4, 7)
        start(sides(k, 1))
        sweep(k, 7, BLOCKS)
        start(sides(k, 2))

    def halos(k):
        finish(faces(k)[:2])
        hi, lo = split(xrec[k].reshape(2 * B, B))
        g = dot(jnp.concatenate([hi, lo], axis=1), wy[...])
        hi, lo = split(g[:, :B] + g[:, B:])
        o = dot(bx[...], jnp.concatenate([hi, lo], axis=1))
        o = o[: 2 * B, :B] + o[: 2 * B, B:] + o[2 * B :, :B]
        o = o.reshape(2, CZ, R, B)
        nl[:, 0:R, :] += o[0]
        nl[:, B - R :, :] += o[1]
        finish(faces(k)[2:])
        for c in range(3):
            finish(sides(k, c))
        hi, lo = split(jnp.concatenate([hrec[k, 0], hrec[k, 1]], axis=1))
        yh = dot(hi, by[0]) + dot(lo, by[0]) + dot(hi, by[1])
        hi, lo = split(yh)
        yhi[0 : B + 2 * R, :] = hi
        ylo[0 : B + 2 * R, :] = lo
        both = dot(ae[...], yhi[...])
        hout[...] = both[:B] + both[B:] + dot(ae[:B, :], ylo[...])

    for k in range(OUTER):
        sweep_all(k)
        own_part(k)
        halos(k)

    def stress(left, goal, p):
        return left * ((goal + SHIFT) * 0.5 - p)

    both = jnp.logical_and
    ends = [
        (rt, lf, rdma(OUTER, 0, fpack, frec.at[R:, :], 0, 1)),
        (both(dn, rt), both(up, lf), rdma(OUTER, 2, fpack.at[B - R :, :], frec.at[:R, :], 1, 1)),
        (dn, up, rdma(OUTER, 1, se.at[:, B + R - 1 : B + R, :], se.at[:, R - 1 : R, :], 1, 0)),
    ]

    def last(i, carry):
        for at in rows_of(i):
            inside = pl.ds(pl.multiple_of(at.start + R, R), R)
            for z in range(CZ):
                left = damage_left(z, at)
                d_o[z, at, :] = 1.0 - left
                here = stress(left, g_v[z, at, :], p_o[z, at, :])
                se[z, inside, :] = here
                turned = pltpu.roll(here, z + 1, 1)
                acc = turned if z == 0 else jnp.where(lane == z, turned, acc)
            fpack[at, :] = acc

        return carry

    lax.fori_loop(0, 1, last, 0)
    start(ends[2:])
    lax.fori_loop(1, BLOCKS, last, 0)
    start(ends[:2])
    row8 = lax.broadcasted_iota(jnp.int32, (R, B), 0)

    def inner_forces(z, carry):
        prev = None
        for i in range(1, B // R + 1):
            at = slice(R * i, R * i + R)
            s = se[z, at, :]
            l = jnp.where(lane == 0, 0.0, pltpu.roll(s, 1, 1))
            total, other = l + s, l - s
            if prev is None:
                sum_up = jnp.where(row8 == 0, 0.0, pltpu.roll(total, 1, 0))
                dif_up = jnp.where(row8 == 0, 0.0, pltpu.roll(other, 1, 0))
            else:
                sum_up = pltpu.roll(jnp.where(row8 == R - 1, prev[0], total), 1, 0)
                dif_up = pltpu.roll(jnp.where(row8 == R - 1, prev[1], other), 1, 0)
            f_o[0, z, R * i - R : R * i, :] = 0.5 * (sum_up - total)
            f_o[1, z, R * i - R : R * i, :] = 0.5 * (dif_up + other)
            prev = total, other
        return carry

    lax.fori_loop(0, CZ, inner_forces, 0)
    finish(ends)


def forces(se, frec, p_v, d_v, f_i, p_h, d_h, f_h, f_v, sem):
    copies = [pltpu.make_async_copy(p_v, p_h, sem.at[0]), pltpu.make_async_copy(d_v, d_h, sem.at[1])]
    for copy in copies:
        copy.start()
    lane8 = lax.broadcasted_iota(jnp.int32, (R, B), 1)
    row8 = lax.broadcasted_iota(jnp.int32, (R, B), 0)
    first = lane8 == 0
    sides = []
    for i in range(1, B // R + 1):
        col, before = frec[R * i : R * i + R, :], frec[R * i - R : R * i, :]
        up = pltpu.roll(jnp.where(row8 == R - 1, before, col), 1, 0)
        sides.append((0.5 * (up - col), 0.5 * (up + col)))
    for z in range(CZ):
        for i in range(B // R):
            at = slice(R * i, R * i + R)
            for c in range(2):
                part = sides[i][c]
                if z:
                    part = pltpu.roll(part, 128 - z, 1)
                f = f_i[c, z, at, :] + jnp.where(first, part, 0.0)
                if i == 0:
                    u = pltpu.roll(se[z, 0:R, :], 1, 0)
                    left = jnp.where(first, 0.0, pltpu.roll(u, 1, 1))
                    edge = 0.5 * (u + left) if c == 0 else 0.5 * (left - u)
                    f = f + jnp.where(row8 == 0, edge, 0.0)
                f_v[c, z, at, :] = f
        for c in range(2):
            copies.append(pltpu.make_async_copy(f_v.at[c, z], f_h.at[c, z], sem.at[2 + 2 * z + c]))
            copies[-1].start()
    for copy in copies:
        copy.wait()


def solution(mesh):
    nx, ny = mesh.shape["gx"], mesh.shape["gy"]
    consts = tables()
    hbm = pl.BlockSpec(memory_space=pltpu.MemorySpace.HBM)
    vmem = pl.BlockSpec(memory_space=pltpu.MemorySpace.VMEM)
    block = jax.ShapeDtypeStruct((CZ, B, B), F32)
    scratch = [
        pltpu.VMEM((CZ, B, B), F32),
        pltpu.VMEM((CZ, B, B), F32),
        pltpu.VMEM((CZ, B, B), jnp.int32),
        pltpu.VMEM((CZ, B, B), jnp.int32),
        pltpu.VMEM((CZ, B, B), F32),
        pltpu.VMEM((CZ, B, B), F32),
        pltpu.VMEM((OUTER - 1, CZ, B, B), F32),
        pltpu.VMEM((CZ, B, B), F32),
        pltpu.VMEM((CZ // 2, 2 * B, 2 * B), BF16),
        pltpu.VMEM((CZ, B, B), F32),
        pltpu.VMEM((B, 2 * B), F32),
        pltpu.VMEM((2 * B, 2 * B), BF16),
        pltpu.VMEM((2 * B, 2 * B), BF16),
        pltpu.VMEM((OUTER, 2, B, B), F32),
        pltpu.VMEM((OUTER, 2, B + 2 * R, B), F32),
        pltpu.VMEM((OUTER, 2, CZ, R, B), F32),
        pltpu.VMEM((2 * B, 2 * B), BF16),
        pltpu.VMEM((2 * B, 2 * B), BF16),
        pltpu.VMEM((2 * B, 2 * B), BF16),
        pltpu.VMEM((2, 2 * B, 2 * B), BF16),
        pltpu.VMEM((4 * B, 2 * B), BF16),
        pltpu.VMEM((B, B), F32),
        pltpu.SemaphoreType.DMA((4, 4)),
        pltpu.SemaphoreType.DMA((6,)),
        pltpu.SemaphoreType.DMA((OUTER + 1, 14)),
        pltpu.SemaphoreType.DMA((OUTER + 1, 14)),
    ]

    def local(*args):
        p, d, f, stress, column = pl.pallas_call(
            functools.partial(kernel, nx, ny),
            out_shape=(
                block,
                block,
                jax.ShapeDtypeStruct((2, CZ, B, B), F32),
                jax.ShapeDtypeStruct((CZ, B + R, B), F32),
                jax.ShapeDtypeStruct((B + R, B), F32),
            ),
            in_specs=[hbm] * 10,
            out_specs=[vmem] * 5,
            scratch_shapes=scratch,
            compiler_params=pltpu.CompilerParams(
                collective_id=0, has_side_effects=True, vmem_limit_bytes=KERNEL_VMEM
            ),
        )(*[pltpu.with_memory_space_constraint(a, pltpu.MemorySpace.HBM) for a in (*args, *[jnp.asarray(c) for c in consts])])
        return pl.pallas_call(
            forces,
            out_shape=(block, block, jax.ShapeDtypeStruct((2, CZ, B, B), F32)),
            in_specs=[vmem] * 5,
            out_specs=[hbm] * 3,
            scratch_shapes=[pltpu.VMEM((2, CZ, B, B), F32), pltpu.SemaphoreType.DMA((2 + 2 * CZ,))],
            compiler_params=pltpu.CompilerParams(vmem_limit_bytes=FORCE_VMEM),
        )(stress, column, p, d, f)

    placed = P(None, "gx", "gy")
    return jax.shard_map(
        local,
        mesh=mesh,
        in_specs=(placed,) * 5,
        out_specs=(placed, placed, P(None, None, "gx", "gy")),
        check_vma=False,
    )
```

```python
import functools
import math

import jax
import jax.numpy as jnp
import numpy as np
from jax import lax
from jax.experimental import pallas as pl
from jax.experimental.pallas import tpu as pltpu
from jax.sharding import PartitionSpec as P

NEWTON_MAX = 6
OUTER = 3
CZ = 16
B = 128
R = 8
ROWS = 16
BLOCKS = B // ROWS
LOG2E = 1.0 / math.log(2.0)
SHIFT = 0.5 * math.log(2.0)
F32 = jnp.float32
BF16 = jnp.bfloat16
MESH = pl.DeviceIdType.MESH


def tap(t):
    t = np.asarray(t, np.float64)
    return np.where(np.abs(t) <= R, np.exp(-t * t / 32.0), 0.0)


def two(m):
    hi = np.asarray(m, np.float64).astype(BF16)
    lo = (m - hi.astype(np.float64)).astype(BF16)
    return hi, lo


def axis_norm(first, last, n):
    at = np.arange(n)
    norm = np.zeros(n)
    for off in range(-R, R + 1):
        to = at + off
        inside = np.ones(n, bool)
        if first:
            inside &= to >= 0
        if last:
            inside &= to < n
        norm += np.where(inside, tap(off), 0.0)
    return norm


def axis_matrix(first, last):
    out = np.arange(B)[:, None]
    col = np.arange(B + 2 * R)[None, :] - R
    return tap(out - col) / axis_norm(first, last, B)[:, None]


def depth_matrix():
    at = np.arange(CZ)
    return tap(at[:, None] - at[None, :]) / axis_norm(True, True, CZ)[:, None]


def tables():
    wy, wx, ae = [], [], []
    full = np.exp(-(np.arange(-R, R + 1) ** 2) / 32.0).sum()
    for first, last in ((True, False), (False, False), (False, True)):
        ext = axis_matrix(first, last)
        own = ext[:, R : R + B]
        hi, lo = two(own.T)
        wy.append(np.block([[hi, lo], [hi, lo]]))
        hi, lo = two(own)
        wx.append(np.block([[hi, hi], [lo, lo]]))
        wide = np.zeros((B + R, 2 * B))
        wide[:B, R : B + 3 * R] = ext
        wide[B + R - 1, : B + 4 * R] = tap(np.arange(B + 4 * R) - 2 * R + 1) / full
        ae.append(np.concatenate(two(wide), axis=0))
    az = depth_matrix()
    by = np.zeros((2 * B, 2 * B))
    bm = np.zeros((B, 2 * B))
    bx = np.zeros((2 * B, 2 * B))
    for z in range(CZ):
        for j in range(R):
            lane = 16 * (z % 8) + 8 * (z // 8) + j
            for zo in range(CZ):
                bm[8 * zo + 7, 8 * z + j] = az[zo, z] * tap(j - 7) / full
                if j == 0:
                    bm[8 * zo + 7, B + 8 * z] = az[zo, z] * tap(8) / full
                base = 128 * (zo // 8) + 16 * (zo % 8)
                for r in range(R):
                    by[lane, base + 8 + r] = az[zo, z] * tap(r - (j - 8)) / full
                    by[B + lane, base + r] = az[zo, z] * tap(r - 8 - j) / full
                    bx[8 * zo + r, 8 * z + j] = az[zo, z] * tap(r - (j - 8)) / full
                    bx[B + 8 * zo + r, B + 8 * z + j] = az[zo, z] * tap(r - 8 - j) / full
    return (
        np.stack(wy),
        np.stack(wx),
        np.stack(ae),
        np.stack(two(by)),
        np.concatenate(two(bx), axis=0),
        np.concatenate(two(bm), axis=0),
    )


def split(v):
    hi = v.astype(BF16)
    return hi, (v - hi.astype(F32)).astype(BF16)


def dot(a, b):
    return jnp.dot(a, b, preferred_element_type=F32)


def newton(start, goal, beta, count):
    y = start
    for s in range(1, NEWTON_MAX + 1):
        moved = y * (0.8 - 0.2 * jnp.tanh(goal - y)) - beta
        y = moved if s <= 3 else jnp.where(count >= s, moved, y)
    return 0.5 * (goal - y) + 0.5 * SHIFT


def depth_halves():
    az = depth_matrix()
    return 0.5 * (az[:8, :8] + az[:8, :7:-1]), 0.5 * (az[:8, :8] - az[:8, :7:-1])


def smooth_depth(planes):
    even, odd = depth_halves()
    add = [planes[z] + planes[CZ - 1 - z] for z in range(8)]
    sub = [planes[z] - planes[CZ - 1 - z] for z in range(8)]
    out = [None] * CZ
    for z in range(8):
        e = float(even[z, 0]) * add[0]
        o = float(odd[z, 0]) * sub[0]
        for i in range(1, 8):
            e = e + float(even[z, i]) * add[i]
            o = o + float(odd[z, i]) * sub[i]
        out[z] = e + o
        out[CZ - 1 - z] = e - o
    return out


KERNEL_VMEM = 30 << 20
FORCE_VMEM = 12 << 20
CHUNKS = ((0, 8), (120, 8), (8, 48), (56, 64))
SIDES = ((0, 56), (56, 48), (104, 24))


def kernel(
    nx, ny,
    t_h, old_h, mask_h, cnt_h, thr_h, wy_h, wx_h, ae_h, by_h, bx_h, bm_h,
    p_o, d_o, f_o, se, frec,
    t_v, old_v, mask_v, cnt_v, thr_v, g_v, p_s, zhl, t2, nl, hout, yhi, ylo, pack, hrec, xrec,
    wy, wx, ae, by, bx, bm, fpack, fold, nine, trow, grow,
    in_sem, w_sem, send, recv,
):
    gx = lax.axis_index("gx")
    gy = lax.axis_index("gy")
    p_v = [p_s.at[0], p_s.at[1], p_o]
    up, dn, lf, rt = gx > 0, gx < nx - 1, gy > 0, gy < ny - 1

    def variant(i, n):
        return jnp.where(i == 0, 0, jnp.where(i == n - 1, 2, 1))

    ins = ((t_h, t_v), (old_h, old_v), (mask_h, mask_v), (cnt_h, cnt_v), (thr_h, thr_v))
    loads = []
    for c, (r0, n) in enumerate(CHUNKS):
        for a, (src, dst) in enumerate(ins[:4]):
            copy = pltpu.make_async_copy(src.at[:, r0 : r0 + n, :], dst.at[:, r0 : r0 + n, :], in_sem.at[c, a])
            copy.start()
            loads.append(copy)
    weights = [
        pltpu.make_async_copy(wy_h.at[variant(gy, ny)], wy, w_sem.at[0]),
        pltpu.make_async_copy(wx_h.at[variant(gx, nx)], wx, w_sem.at[1]),
        pltpu.make_async_copy(ae_h.at[variant(gx, nx)], ae, w_sem.at[2]),
        pltpu.make_async_copy(by_h, by, w_sem.at[3]),
        pltpu.make_async_copy(bx_h, bx, w_sem.at[4]),
        pltpu.make_async_copy(bm_h, bm, w_sem.at[6]),
        pltpu.make_async_copy(thr_h, thr_v, w_sem.at[5]),
    ]
    for copy in weights:
        copy.start()

    barrier = pltpu.get_barrier_semaphore()
    for dx in (-1, 0, 1):
        for dy in (-1, 0, 1):
            if dx == 0 and dy == 0:
                continue
            here = [c for c, on in ((up, dx < 0), (dn, dx > 0), (lf, dy < 0), (rt, dy > 0)) if on]

            @pl.when(functools.reduce(jnp.logical_and, here))
            def _(dx=dx, dy=dy):
                pl.semaphore_signal(barrier, inc=1, device_id=(gx + dx, gy + dy), device_id_type=MESH)

    one = jnp.int32(1)
    zero = jnp.int32(0)
    across = jnp.where(up, one, zero) + jnp.where(dn, one, zero) + 1
    along = jnp.where(lf, one, zero) + jnp.where(rt, one, zero) + 1

    def enter():
        pl.semaphore_wait(barrier, across * along - 1)

    @pl.when(jnp.logical_not(up))
    def _():
        for k in range(OUTER):
            xrec[k, 0] = jnp.zeros((CZ, R, B), F32)
            hrec[k, :, R : 2 * R, :] = jnp.zeros((2, R, B), F32)
        hrec[OUTER - 1, :, 0:R, :] = jnp.zeros((2, R, B), F32)
        se[:, 0:R, :] = jnp.zeros((CZ, R, B), F32)
        fpack[0:R, :] = jnp.zeros((R, B), F32)

    @pl.when(jnp.logical_not(dn))
    def _():
        for k in range(OUTER):
            xrec[k, 1] = jnp.zeros((CZ, R, B), F32)
            hrec[k, :, 2 * R + B : 3 * R + B, :] = jnp.zeros((2, R, B), F32)

    @pl.when(jnp.logical_not(lf))
    def _():
        for k in range(OUTER):
            hrec[k, 0] = jnp.zeros((B + 4 * R, B), F32)
        frec[...] = jnp.zeros((3 * R, B), F32)

    @pl.when(jnp.logical_not(rt))
    def _():
        for k in range(OUTER):
            hrec[k, 1] = jnp.zeros((B + 4 * R, B), F32)

    for k in range(OUTER):
        hrec[k, :, 3 * R + B :, :] = jnp.zeros((2, R, B), F32)
        if k < OUTER - 1:
            hrec[k, :, 0:R, :] = jnp.zeros((2, R, B), F32)
    nine[:, 1:, :] = jnp.zeros((CZ, R - 1, B), F32)
    trow[:, : R - 1, :] = jnp.zeros((CZ, R - 1, B), F32)
    grow[:, : R - 1, :] = jnp.zeros((CZ, R - 1, B), F32)
    yhi[...] = jnp.zeros_like(yhi)
    ylo[...] = jnp.zeros_like(ylo)

    lane = lax.broadcasted_iota(jnp.int32, (R, B), 1)
    slot = lane // 16
    low = (lane % 16) < 8
    row8 = lax.broadcasted_iota(jnp.int32, (R, B), 0)
    total = math.fsum(math.exp(-(t * t) / 32.0) for t in range(-R, R + 1))
    after_one = (row8 + 1).astype(F32)
    reach = jnp.exp(after_one * after_one * (-1.0 / 32.0)) * (1.0 / total)
    rim = jnp.logical_or(lane < R, lane >= B - R)

    def rdma(k, i, src, dst, dx, dy):
        ix = jnp.clip(gx + dx, 0, nx - 1)
        iy = jnp.clip(gy + dy, 0, ny - 1)
        return pltpu.make_async_remote_copy(
            src_ref=src, dst_ref=dst, send_sem=send.at[k, i], recv_sem=recv.at[k, i],
            device_id=(ix, iy), device_id_type=MESH,
        )

    def faces(k):
        both = jnp.logical_and
        top, bottom = slice(0, R), slice(B - R, B)
        after = slice(2 * R + B, 3 * R + B)
        deep = 2 * R if k == OUTER - 1 else R
        tail, ahead = slice(B - deep, B), slice(2 * R - deep, 2 * R)
        return [
            (up, dn, rdma(k, 0, p_v[k].at[:, top, :], xrec.at[k, 1], -1, 0)),
            (dn, up, rdma(k, 1, p_v[k].at[:, bottom, :], xrec.at[k, 0], 1, 0)),
            (both(dn, rt), both(up, lf), rdma(k, 2, pack.at[k, 1, tail], hrec.at[k, 0, ahead], 1, 1)),
            (both(up, rt), both(dn, lf), rdma(k, 3, pack.at[k, 1, top], hrec.at[k, 0, after], -1, 1)),
            (both(dn, lf), both(up, rt), rdma(k, 4, pack.at[k, 0, tail], hrec.at[k, 1, ahead], 1, -1)),
            (both(up, lf), both(dn, rt), rdma(k, 5, pack.at[k, 0, top], hrec.at[k, 1, after], -1, -1)),
        ]

    def sides(k, c):
        r0, n = SIDES[c]
        here, there = slice(r0, r0 + n), slice(2 * R + r0, 2 * R + r0 + n)
        return [
            (rt, lf, rdma(k, 6 + 2 * c, pack.at[k, 1, here], hrec.at[k, 0, there], 0, 1)),
            (lf, rt, rdma(k, 7 + 2 * c, pack.at[k, 0, here], hrec.at[k, 1, there], 0, -1)),
        ]

    def statics():
        return [
            (dn, up, rdma(OUTER, 1, g_v.at[:, B - 1 : B, :], grow.at[:, R - 1 : R, :], 1, 0)),
            (dn, up, rdma(OUTER, 2, thr_v.at[:, B - 1 : B, :], trow.at[:, R - 1 : R, :], 1, 0)),
        ]

    def ninth():
        last = OUTER - 1
        return [(dn, up, rdma(OUTER, 3, p_v[last].at[:, B - R - 1 : B - R, :], nine.at[:, 0:1, :], 1, 0))]

    def start(copies):
        for sends, _, copy in copies:
            pl.when(sends)(copy.start)

    def finish(copies):
        for sends, gets, copy in copies:
            pl.when(gets)(copy.wait_recv)
            pl.when(sends)(copy.wait_send)

    def rows_of(i):
        first = jnp.where(i == 0, 0, ROWS * i - R)
        second = jnp.where(i == 0, B - R, ROWS * i)
        return [pl.ds(pl.multiple_of(first, R), R), pl.ds(pl.multiple_of(second, R), R)]

    def packed(read):
        halves = []
        for h in range(2):
            acc = None
            for zz in range(8):
                turned = pltpu.roll(read(8 * h + zz), (16 * zz + 8) % 128, 1)
                acc = turned if acc is None else jnp.where(slot == zz, turned, acc)
            halves.append(acc)
        return interleave(*halves)

    def interleave(a, b):
        return jnp.where(low, pltpu.roll(a, 120, 1), b), jnp.where(low, a, pltpu.roll(b, 8, 1))

    def halo_add(z, at):
        return nl[z, at, :] + halo_part(z, at)

    def halo_part(z, at):
        h, zz = z // 8, z % 8
        part = pltpu.roll(hout[at, 128 * h : 128 * h + 128], (120 - 16 * zz) % 128, 1)
        return jnp.where(rim, part, 0.0)

    def damage_left(z, at):
        return decay(halo_add(z, at), thr_v[z, at, :])

    def solve(start, goal, old, count, left):
        beta = 0.2 if left is None else 0.1 * left + 0.1
        reach = 17.5 * beta
        return jnp.where(count > 0, newton(start - reach, goal - reach, beta, count), old)

    def decay(average, threshold):
        return jnp.exp2(jnp.maximum(average - threshold, 0.0) * (-LOG2E / 0.3))

    def update(k, i):
        for at in rows_of(i):
            for z in range(CZ):
                if k == 0:
                    t, old = t_v[z, at, :], old_v[z, at, :]
                    count = mask_v[z, at, :] * cnt_v[z, at, :]
                    cnt_v[z, at, :] = count
                    goal = 2.0 * (t + old) - SHIFT
                    start = 2.0 * t
                    g_v[z, at, :] = goal
                    t_v[z, at, :] = start
                    left = None
                else:
                    start, goal, old, count = t_v[z, at, :], g_v[z, at, :], old_v[z, at, :], cnt_v[z, at, :]
                    left = damage_left(z, at)
                p_v[k][z, at, :] = solve(start, goal, old, count, left)
            pack[k, 0, at, :], pack[k, 1, at, :] = packed(lambda z: p_v[k][z, at, :])

    def own_part(k):
        def depth(i, carry):
            at8 = pl.ds(pl.multiple_of(i * R, R), R)
            for z, plane in enumerate(smooth_depth([p_v[k][z, at8, :] for z in range(CZ)])):
                zhl[z, at8, :] = plane
            return carry

        lax.fori_loop(0, B // R, depth, 0)
        for b in range(BLOCKS):
            hi, lo = split(zhl[:, ROWS * b : ROWS * b + ROWS, :].reshape(CZ * ROWS, B))
            t = dot(jnp.concatenate([hi, lo], axis=1), wy[...])
            hi, lo = split(t[:, :B] + t[:, B:])
            for z in range(CZ):
                half, rows = slice(128 * (z % 2), 128 * (z % 2) + 128), slice(ROWS * z, ROWS * z + ROWS)
                t2[z // 2, ROWS * b : ROWS * b + ROWS, half] = hi[rows]
                t2[z // 2, B + ROWS * b : B + ROWS * b + ROWS, half] = lo[rows]
        for i in range(CZ // 2):
            o = dot(wx[...], t2[i])
            o = o[:B] + o[B:]
            nl[2 * i] = o[:, :B]
            nl[2 * i + 1] = o[:, B:]

    def sweep(k, lo, hi):
        def body(i, carry):
            update(k, i)
            return carry

        lax.fori_loop(lo, hi, body, 0)

    def arrived(c):
        for copy in loads[4 * c : 4 * c + 4]:
            copy.wait()

    def sweep_all(k):
        if k == 0:
            arrived(0)
            arrived(1)
        sweep(k, 0, 1)
        if k == 0:
            enter()
        if k < OUTER - 1:
            start(faces(k))
        else:
            start(faces(k)[:2])
            sweep(k, 7, BLOCKS)
            start(ninth())
            start(faces(k)[2:])
            start(sides(k, 2))
        if k == 0:
            arrived(2)
        sweep(k, 1, 4)
        start(sides(k, 0))
        if k == 0:
            arrived(3)
            for copy in weights:
                copy.wait()
            start(statics())
        sweep(k, 4, 7)
        start(sides(k, 1))
        if k < OUTER - 1:
            sweep(k, 7, BLOCKS)
            start(sides(k, 2))

    def halos(k):
        finish(faces(k)[:2])
        hi, lo = split(xrec[k].reshape(2 * B, B))
        g = dot(jnp.concatenate([hi, lo], axis=1), wy[...])
        hi, lo = split(g[:, :B] + g[:, B:])
        o = dot(bx[...], jnp.concatenate([hi, lo], axis=1))
        o = o[: 2 * B, :B] + o[: 2 * B, B:] + o[2 * B :, :B]
        o = o.reshape(2, CZ, R, B)
        nl[:, 0:R, :] += o[0]
        nl[:, B - R :, :] += o[1]
        if k == OUTER - 1:
            finish(ninth())
            n_hi, n_lo = split(nine[...].reshape(B, B))
            n = dot(jnp.concatenate([n_hi, n_lo], axis=1), wy[...])
            n_hi, n_lo = split(n[:, :B] + n[:, B:])
            o = dot(
                bm[...],
                jnp.concatenate(
                    [jnp.concatenate([hi[:B], lo[:B]], axis=1), jnp.concatenate([n_hi, n_lo], axis=1)], axis=0
                ),
            )
            o = o[:B, :B] + o[:B, B:] + o[B:, :B]
            for z in range(CZ):
                half = slice(128 * (z % 2), 128 * (z % 2) + 128)
                own = t2[z // 2, 0:ROWS, half].astype(F32) + t2[z // 2, B : B + ROWS, half].astype(F32)
                own = jnp.sum(own[:R] * reach, axis=0, keepdims=True)
                nine[z] = o[R * z : R * z + R] + jnp.where(row8 == R - 1, own, 0.0)
        finish(faces(k)[2:])
        for c in range(3):
            finish(sides(k, c))
        hi, lo = split(jnp.concatenate([hrec[k, 0], hrec[k, 1]], axis=1))
        yh = dot(hi, by[0]) + dot(lo, by[0]) + dot(hi, by[1])
        hi, lo = split(yh)
        yhi[0 : B + 4 * R, :] = hi
        ylo[0 : B + 4 * R, :] = lo
        both = dot(ae[...], yhi[...])
        hout[...] = both[: B + R] + both[B + R :] + dot(ae[: B + R, :], ylo[...])

    for k in range(OUTER):
        sweep_all(k)
        own_part(k)
        halos(k)

    def stress(left, goal, p):
        return left * ((goal + SHIFT) * 0.5 - p)

    ends = [(rt, lf, rdma(OUTER, 0, fold, frec, 0, 1))]
    finish(statics())

    @pl.when(up)
    def _():
        for z in range(CZ):
            left = decay(nine[z] + halo_part(z, slice(B, B + R)), trow[z])
            here = stress(left, grow[z], xrec[OUTER - 1, 0, z])
            se[z, 0:R, :] = here
            turned = pltpu.roll(here, z + 1, 1)
            acc = turned if z == 0 else jnp.where(lane == z, turned, acc)
        fpack[0:R, :] = acc

    def last(i, carry):
        for at in rows_of(i):
            inside = pl.ds(pl.multiple_of(at.start + R, R), R)
            for z in range(CZ):
                left = damage_left(z, at)
                d_o[z, at, :] = 1.0 - left
                here = stress(left, g_v[z, at, :], p_o[z, at, :])
                se[z, inside, :] = here
                turned = pltpu.roll(here, z + 1, 1)
                acc = turned if z == 0 else jnp.where(lane == z, turned, acc)
            fpack[inside, :] = acc

        return carry

    lax.fori_loop(0, BLOCKS, last, 0)
    fold[0:R, :] = fpack[0:R, :]
    for h in range(2):
        acc = None
        for i in range(8):
            part = fpack[R * (8 * h + i + 1) : R * (8 * h + i + 2), :]
            acc = part if i == 0 else jnp.where(slot == i, pltpu.roll(part, 16 * i, 1), acc)
        fold[R * (h + 1) : R * (h + 2), :] = acc
    start(ends)

    def inner_forces(z, carry):
        prev = None
        for i in range(1, B // R + 1):
            at = slice(R * i, R * i + R)
            s = se[z, at, :]
            l = jnp.where(lane == 0, 0.0, pltpu.roll(s, 1, 1))
            total, other = l + s, l - s
            if prev is None:
                sum_up = jnp.where(row8 == 0, 0.0, pltpu.roll(total, 1, 0))
                dif_up = jnp.where(row8 == 0, 0.0, pltpu.roll(other, 1, 0))
            else:
                sum_up = pltpu.roll(jnp.where(row8 == R - 1, prev[0], total), 1, 0)
                dif_up = pltpu.roll(jnp.where(row8 == R - 1, prev[1], other), 1, 0)
            f_o[0, z, R * i - R : R * i, :] = 0.5 * (sum_up - total)
            f_o[1, z, R * i - R : R * i, :] = 0.5 * (dif_up + other)
            prev = total, other
        return carry

    lax.fori_loop(0, CZ, inner_forces, 0)
    finish(ends)


def forces(se, frec, p_v, d_v, f_i, p_h, d_h, f_h, f_v, sem):
    copies = [pltpu.make_async_copy(p_v, p_h, sem.at[0]), pltpu.make_async_copy(d_v, d_h, sem.at[1])]
    for copy in copies:
        copy.start()
    lane8 = lax.broadcasted_iota(jnp.int32, (R, B), 1)
    row8 = lax.broadcasted_iota(jnp.int32, (R, B), 0)
    first = lane8 == 0
    sides = []
    cols = [frec[0:R, :]]
    for i in range(B // R):
        col = frec[R * (i // 8 + 1) : R * (i // 8 + 2), :]
        cols.append(pltpu.roll(col, 128 - 16 * (i % 8), 1) if i % 8 else col)
    for i in range(1, B // R + 1):
        col, before = cols[i], cols[i - 1]
        up = pltpu.roll(jnp.where(row8 == R - 1, before, col), 1, 0)
        sides.append((0.5 * (up - col), 0.5 * (up + col)))
    for z in range(CZ):
        for i in range(B // R):
            at = slice(R * i, R * i + R)
            for c in range(2):
                part = sides[i][c]
                if z:
                    part = pltpu.roll(part, 128 - z, 1)
                f = f_i[c, z, at, :] + jnp.where(first, part, 0.0)
                if i == 0:
                    u = pltpu.roll(se[z, 0:R, :], 1, 0)
                    left = jnp.where(first, 0.0, pltpu.roll(u, 1, 1))
                    edge = 0.5 * (u + left) if c == 0 else 0.5 * (left - u)
                    f = f + jnp.where(row8 == 0, edge, 0.0)
                f_v[c, z, at, :] = f
        for c in range(2):
            copies.append(pltpu.make_async_copy(f_v.at[c, z], f_h.at[c, z], sem.at[2 + 2 * z + c]))
            copies[-1].start()
    for copy in copies:
        copy.wait()


def solution(mesh):
    nx, ny = mesh.shape["gx"], mesh.shape["gy"]
    consts = tables()
    hbm = pl.BlockSpec(memory_space=pltpu.MemorySpace.HBM)
    vmem = pl.BlockSpec(memory_space=pltpu.MemorySpace.VMEM)
    block = jax.ShapeDtypeStruct((CZ, B, B), F32)
    scratch = [
        pltpu.VMEM((CZ, B, B), F32),
        pltpu.VMEM((CZ, B, B), F32),
        pltpu.VMEM((CZ, B, B), jnp.int32),
        pltpu.VMEM((CZ, B, B), jnp.int32),
        pltpu.VMEM((CZ, B, B), F32),
        pltpu.VMEM((CZ, B, B), F32),
        pltpu.VMEM((OUTER - 1, CZ, B, B), F32),
        pltpu.VMEM((CZ, B, B), F32),
        pltpu.VMEM((CZ // 2, 2 * B, 2 * B), BF16),
        pltpu.VMEM((CZ, B, B), F32),
        pltpu.VMEM((B + R, 2 * B), F32),
        pltpu.VMEM((2 * B, 2 * B), BF16),
        pltpu.VMEM((2 * B, 2 * B), BF16),
        pltpu.VMEM((OUTER, 2, B, B), F32),
        pltpu.VMEM((OUTER, 2, B + 4 * R, B), F32),
        pltpu.VMEM((OUTER, 2, CZ, R, B), F32),
        pltpu.VMEM((2 * B, 2 * B), BF16),
        pltpu.VMEM((2 * B, 2 * B), BF16),
        pltpu.VMEM((2 * B + 2 * R, 2 * B), BF16),
        pltpu.VMEM((2, 2 * B, 2 * B), BF16),
        pltpu.VMEM((4 * B, 2 * B), BF16),
        pltpu.VMEM((2 * B, 2 * B), BF16),
        pltpu.VMEM((B + R, B), F32),
        pltpu.VMEM((3 * R, B), F32),
        pltpu.VMEM((CZ, R, B), F32),
        pltpu.VMEM((CZ, R, B), F32),
        pltpu.VMEM((CZ, R, B), F32),
        pltpu.SemaphoreType.DMA((4, 4)),
        pltpu.SemaphoreType.DMA((7,)),
        pltpu.SemaphoreType.DMA((OUTER + 1, 14)),
        pltpu.SemaphoreType.DMA((OUTER + 1, 14)),
    ]

    def local(*args):
        p, d, f, stress, column = pl.pallas_call(
            functools.partial(kernel, nx, ny),
            out_shape=(
                block,
                block,
                jax.ShapeDtypeStruct((2, CZ, B, B), F32),
                jax.ShapeDtypeStruct((CZ, B + R, B), F32),
                jax.ShapeDtypeStruct((3 * R, B), F32),
            ),
            in_specs=[hbm] * 11,
            out_specs=[vmem] * 5,
            scratch_shapes=scratch,
            compiler_params=pltpu.CompilerParams(
                collective_id=0, has_side_effects=True, vmem_limit_bytes=KERNEL_VMEM
            ),
        )(*[pltpu.with_memory_space_constraint(a, pltpu.MemorySpace.HBM) for a in (*args, *[jnp.asarray(c) for c in consts])])
        return pl.pallas_call(
            forces,
            out_shape=(block, block, jax.ShapeDtypeStruct((2, CZ, B, B), F32)),
            in_specs=[vmem] * 5,
            out_specs=[hbm] * 3,
            scratch_shapes=[pltpu.VMEM((2, CZ, B, B), F32), pltpu.SemaphoreType.DMA((2 + 2 * CZ,))],
            compiler_params=pltpu.CompilerParams(vmem_limit_bytes=FORCE_VMEM),
        )(stress, column, p, d, f)

    placed = P(None, "gx", "gy")
    return jax.shard_map(
        local,
        mesh=mesh,
        in_specs=(placed,) * 5,
        out_specs=(placed, placed, P(None, None, "gx", "gy")),
        check_vma=False,
    )
```

```python
import functools
import math

import jax
import jax.numpy as jnp
import numpy as np
from jax import lax
from jax.experimental import pallas as pl
from jax.experimental.pallas import tpu as pltpu
from jax.sharding import PartitionSpec as P

NEWTON_MAX = 6
OUTER = 3
CZ = 16
B = 128
R = 8
ROWS = 16
BLOCKS = B // ROWS
LOG2E = 1.0 / math.log(2.0)
SHIFT = 0.5 * math.log(2.0)
F32 = jnp.float32
BF16 = jnp.bfloat16
MESH = pl.DeviceIdType.MESH


def tap(t):
    t = np.asarray(t, np.float64)
    return np.where(np.abs(t) <= R, np.exp(-t * t / 32.0), 0.0)


def two(m):
    hi = np.asarray(m, np.float64).astype(BF16)
    lo = (m - hi.astype(np.float64)).astype(BF16)
    return hi, lo


def axis_norm(first, last, n):
    at = np.arange(n)
    norm = np.zeros(n)
    for off in range(-R, R + 1):
        to = at + off
        inside = np.ones(n, bool)
        if first:
            inside &= to >= 0
        if last:
            inside &= to < n
        norm += np.where(inside, tap(off), 0.0)
    return norm


def axis_matrix(first, last):
    out = np.arange(B)[:, None]
    col = np.arange(B + 2 * R)[None, :] - R
    return tap(out - col) / axis_norm(first, last, B)[:, None]


def depth_matrix():
    at = np.arange(CZ)
    return tap(at[:, None] - at[None, :]) / axis_norm(True, True, CZ)[:, None]


def tables():
    wy, wx, ae = [], [], []
    full = np.exp(-(np.arange(-R, R + 1) ** 2) / 32.0).sum()
    for first, last in ((True, False), (False, False), (False, True)):
        ext = axis_matrix(first, last)
        own = ext[:, R : R + B]
        hi, lo = two(own.T)
        wy.append(np.block([[hi, lo], [hi, lo]]))
        hi, lo = two(own)
        wx.append(np.block([[hi, hi], [lo, lo]]))
        wide = np.zeros((B + R, 2 * B))
        wide[:B, R : B + 3 * R] = ext
        wide[B + R - 1, : B + 4 * R] = tap(np.arange(B + 4 * R) - 2 * R + 1) / full
        ae.append(np.concatenate(two(wide), axis=0))
    az = depth_matrix()
    by = np.zeros((2 * B, 2 * B))
    bm = np.zeros((B, 2 * B))
    bx = np.zeros((2 * B, 2 * B))
    for z in range(CZ):
        for j in range(R):
            lane = 16 * (z % 8) + 8 * (z // 8) + j
            for zo in range(CZ):
                bm[8 * zo + 7, 8 * z + j] = az[zo, z] * tap(j - 7) / full
                if j == 0:
                    bm[8 * zo + 7, B + 8 * z] = az[zo, z] * tap(8) / full
                base = 128 * (zo // 8) + 16 * (zo % 8)
                for r in range(R):
                    by[lane, base + 8 + r] = az[zo, z] * tap(r - (j - 8)) / full
                    by[B + lane, base + r] = az[zo, z] * tap(r - 8 - j) / full
                    bx[8 * zo + r, 8 * z + j] = az[zo, z] * tap(r - (j - 8)) / full
                    bx[B + 8 * zo + r, B + 8 * z + j] = az[zo, z] * tap(r - 8 - j) / full
    return (
        np.stack(wy),
        np.stack(wx),
        np.stack(ae),
        np.stack(two(by)),
        np.concatenate(two(bx), axis=0),
        np.concatenate(two(bm), axis=0),
    )


def split(v):
    hi = v.astype(BF16)
    return hi, (v - hi.astype(F32)).astype(BF16)


def dot(a, b):
    return jnp.dot(a, b, preferred_element_type=F32)


def newton(start, goal, beta, count):
    y = start
    for s in range(1, NEWTON_MAX + 1):
        moved = y * (0.8 - 0.2 * jnp.tanh(goal - y)) - beta
        y = moved if s <= 3 else jnp.where(count >= s, moved, y)
    return 0.5 * (goal - y) + 0.5 * SHIFT


def depth_halves():
    az = depth_matrix()
    return 0.5 * (az[:8, :8] + az[:8, :7:-1]), 0.5 * (az[:8, :8] - az[:8, :7:-1])


def smooth_depth(planes):
    even, odd = depth_halves()
    add = [planes[z] + planes[CZ - 1 - z] for z in range(8)]
    sub = [planes[z] - planes[CZ - 1 - z] for z in range(8)]
    out = [None] * CZ
    for z in range(8):
        e = float(even[z, 0]) * add[0]
        o = float(odd[z, 0]) * sub[0]
        for i in range(1, 8):
            e = e + float(even[z, i]) * add[i]
            o = o + float(odd[z, i]) * sub[i]
        out[z] = e + o
        out[CZ - 1 - z] = e - o
    return out


KERNEL_VMEM = 30 << 20
FORCE_VMEM = 12 << 20
CHUNKS = ((0, 8), (120, 8), (8, 48), (56, 64))
SIDES = ((0, 56), (56, 32), (104, 24), (88, 16))


def kernel(
    nx, ny,
    t_h, old_h, mask_h, cnt_h, thr_h, wy_h, wx_h, ae_h, by_h, bx_h, bm_h,
    p_o, d_o, f_o, se, frec,
    t_v, old_v, mask_v, cnt_v, thr_v, g_v, p_s, zhl, t2, nl, hout, yhi, ylo, pack, hrec, xrec,
    wy, wx, ae, by, bx, bm, fpack, fold, nine, trow, grow,
    in_sem, w_sem, send, recv,
):
    gx = lax.axis_index("gx")
    gy = lax.axis_index("gy")
    p_v = [p_s.at[0], p_s.at[1], p_o]
    up, dn, lf, rt = gx > 0, gx < nx - 1, gy > 0, gy < ny - 1

    def variant(i, n):
        return jnp.where(i == 0, 0, jnp.where(i == n - 1, 2, 1))

    ins = ((t_h, t_v), (old_h, old_v), (mask_h, mask_v), (cnt_h, cnt_v), (thr_h, thr_v))
    loads = []
    for c, (r0, n) in enumerate(CHUNKS):
        for a, (src, dst) in enumerate(ins[:4]):
            copy = pltpu.make_async_copy(src.at[:, r0 : r0 + n, :], dst.at[:, r0 : r0 + n, :], in_sem.at[c, a])
            copy.start()
            loads.append(copy)
    weights = [
        pltpu.make_async_copy(wy_h.at[variant(gy, ny)], wy, w_sem.at[0]),
        pltpu.make_async_copy(wx_h.at[variant(gx, nx)], wx, w_sem.at[1]),
        pltpu.make_async_copy(ae_h.at[variant(gx, nx)], ae, w_sem.at[2]),
        pltpu.make_async_copy(by_h, by, w_sem.at[3]),
        pltpu.make_async_copy(bx_h, bx, w_sem.at[4]),
        pltpu.make_async_copy(bm_h, bm, w_sem.at[6]),
        pltpu.make_async_copy(thr_h, thr_v, w_sem.at[5]),
    ]
    for copy in weights:
        copy.start()

    barrier = pltpu.get_barrier_semaphore()
    for dx in (-1, 0, 1):
        for dy in (-1, 0, 1):
            if dx == 0 and dy == 0:
                continue
            here = [c for c, on in ((up, dx < 0), (dn, dx > 0), (lf, dy < 0), (rt, dy > 0)) if on]

            @pl.when(functools.reduce(jnp.logical_and, here))
            def _(dx=dx, dy=dy):
                pl.semaphore_signal(barrier, inc=1, device_id=(gx + dx, gy + dy), device_id_type=MESH)

    one = jnp.int32(1)
    zero = jnp.int32(0)
    across = jnp.where(up, one, zero) + jnp.where(dn, one, zero) + 1
    along = jnp.where(lf, one, zero) + jnp.where(rt, one, zero) + 1

    def enter():
        pl.semaphore_wait(barrier, across * along - 1)

    @pl.when(jnp.logical_not(up))
    def _():
        for k in range(OUTER):
            xrec[k, 0] = jnp.zeros((CZ, R, B), F32)
            hrec[k, :, R : 2 * R, :] = jnp.zeros((2, R, B), F32)
        hrec[OUTER - 1, :, 0:R, :] = jnp.zeros((2, R, B), F32)
        se[:, 0:R, :] = jnp.zeros((CZ, R, B), F32)
        fpack[0:R, :] = jnp.zeros((R, B), F32)

    @pl.when(jnp.logical_not(dn))
    def _():
        for k in range(OUTER):
            xrec[k, 1] = jnp.zeros((CZ, R, B), F32)
            hrec[k, :, 2 * R + B : 3 * R + B, :] = jnp.zeros((2, R, B), F32)

    @pl.when(jnp.logical_not(lf))
    def _():
        for k in range(OUTER):
            hrec[k, 0] = jnp.zeros((B + 4 * R, B), F32)
        frec[...] = jnp.zeros((3 * R, B), F32)

    @pl.when(jnp.logical_not(rt))
    def _():
        for k in range(OUTER):
            hrec[k, 1] = jnp.zeros((B + 4 * R, B), F32)

    for k in range(OUTER):
        hrec[k, :, 3 * R + B :, :] = jnp.zeros((2, R, B), F32)
        if k < OUTER - 1:
            hrec[k, :, 0:R, :] = jnp.zeros((2, R, B), F32)
    nine[:, 1:, :] = jnp.zeros((CZ, R - 1, B), F32)
    trow[:, : R - 1, :] = jnp.zeros((CZ, R - 1, B), F32)
    grow[:, : R - 1, :] = jnp.zeros((CZ, R - 1, B), F32)
    yhi[...] = jnp.zeros_like(yhi)
    ylo[...] = jnp.zeros_like(ylo)

    lane = lax.broadcasted_iota(jnp.int32, (R, B), 1)
    slot = lane // 16
    low = (lane % 16) < 8
    row8 = lax.broadcasted_iota(jnp.int32, (R, B), 0)
    total = math.fsum(math.exp(-(t * t) / 32.0) for t in range(-R, R + 1))
    after_one = (row8 + 1).astype(F32)
    reach = jnp.exp(after_one * after_one * (-1.0 / 32.0)) * (1.0 / total)
    rim = jnp.logical_or(lane < R, lane >= B - R)

    def rdma(k, i, src, dst, dx, dy):
        ix = jnp.clip(gx + dx, 0, nx - 1)
        iy = jnp.clip(gy + dy, 0, ny - 1)
        return pltpu.make_async_remote_copy(
            src_ref=src, dst_ref=dst, send_sem=send.at[k, i], recv_sem=recv.at[k, i],
            device_id=(ix, iy), device_id_type=MESH,
        )

    def faces(k):
        both = jnp.logical_and
        top, bottom = slice(0, R), slice(B - R, B)
        after = slice(2 * R + B, 3 * R + B)
        deep = 2 * R if k == OUTER - 1 else R
        tail, ahead = slice(B - deep, B), slice(2 * R - deep, 2 * R)
        return [
            (up, dn, rdma(k, 0, p_v[k].at[:, top, :], xrec.at[k, 1], -1, 0)),
            (dn, up, rdma(k, 1, p_v[k].at[:, bottom, :], xrec.at[k, 0], 1, 0)),
            (both(dn, rt), both(up, lf), rdma(k, 2, pack.at[k, 1, tail], hrec.at[k, 0, ahead], 1, 1)),
            (both(up, rt), both(dn, lf), rdma(k, 3, pack.at[k, 1, top], hrec.at[k, 0, after], -1, 1)),
            (both(dn, lf), both(up, rt), rdma(k, 4, pack.at[k, 0, tail], hrec.at[k, 1, ahead], 1, -1)),
            (both(up, lf), both(dn, rt), rdma(k, 5, pack.at[k, 0, top], hrec.at[k, 1, after], -1, -1)),
        ]

    def sides(k, c):
        r0, n = SIDES[c]
        here, there = slice(r0, r0 + n), slice(2 * R + r0, 2 * R + r0 + n)
        return [
            (rt, lf, rdma(k, 6 + 2 * c, pack.at[k, 1, here], hrec.at[k, 0, there], 0, 1)),
            (lf, rt, rdma(k, 7 + 2 * c, pack.at[k, 0, here], hrec.at[k, 1, there], 0, -1)),
        ]

    def statics():
        return [
            (dn, up, rdma(OUTER, 1, g_v.at[:, B - 1 : B, :], grow.at[:, R - 1 : R, :], 1, 0)),
            (dn, up, rdma(OUTER, 2, thr_v.at[:, B - 1 : B, :], trow.at[:, R - 1 : R, :], 1, 0)),
        ]

    def ninth():
        last = OUTER - 1
        return [(dn, up, rdma(OUTER, 3, p_v[last].at[:, B - R - 1 : B - R, :], nine.at[:, 0:1, :], 1, 0))]

    def start(copies):
        for sends, _, copy in copies:
            pl.when(sends)(copy.start)

    def finish(copies):
        for sends, gets, copy in copies:
            pl.when(gets)(copy.wait_recv)
            pl.when(sends)(copy.wait_send)

    def rows_of(i):
        first = jnp.where(i == 0, 0, ROWS * i - R)
        second = jnp.where(i == 0, B - R, ROWS * i)
        return [pl.ds(pl.multiple_of(first, R), R), pl.ds(pl.multiple_of(second, R), R)]

    def packed(read):
        halves = []
        for h in range(2):
            acc = None
            for zz in range(8):
                turned = pltpu.roll(read(8 * h + zz), (16 * zz + 8) % 128, 1)
                acc = turned if acc is None else jnp.where(slot == zz, turned, acc)
            halves.append(acc)
        return interleave(*halves)

    def interleave(a, b):
        return jnp.where(low, pltpu.roll(a, 120, 1), b), jnp.where(low, a, pltpu.roll(b, 8, 1))

    def halo_add(z, at):
        return nl[z, at, :] + halo_part(z, at)

    def halo_part(z, at):
        h, zz = z // 8, z % 8
        part = pltpu.roll(hout[at, 128 * h : 128 * h + 128], (120 - 16 * zz) % 128, 1)
        return jnp.where(rim, part, 0.0)

    def damage_left(z, at):
        return decay(halo_add(z, at), thr_v[z, at, :])

    def solve(start, goal, old, count, left):
        beta = 0.2 if left is None else 0.1 * left + 0.1
        reach = 17.5 * beta
        return jnp.where(count > 0, newton(start - reach, goal - reach, beta, count), old)

    def decay(average, threshold):
        return jnp.exp2(jnp.maximum(average - threshold, 0.0) * (-LOG2E / 0.3))

    def update(k, i):
        for at in rows_of(i):
            for z in range(CZ):
                if k == 0:
                    t, old = t_v[z, at, :], old_v[z, at, :]
                    count = mask_v[z, at, :] * cnt_v[z, at, :]
                    cnt_v[z, at, :] = count
                    goal = 2.0 * (t + old) - SHIFT
                    start = 2.0 * t
                    g_v[z, at, :] = goal
                    t_v[z, at, :] = start
                    left = None
                else:
                    start, goal, old, count = t_v[z, at, :], g_v[z, at, :], old_v[z, at, :], cnt_v[z, at, :]
                    left = damage_left(z, at)
                p_v[k][z, at, :] = solve(start, goal, old, count, left)
            pack[k, 0, at, :], pack[k, 1, at, :] = packed(lambda z: p_v[k][z, at, :])

    def own_part(k):
        def depth(i, carry):
            at8 = pl.ds(pl.multiple_of(i * R, R), R)
            for z, plane in enumerate(smooth_depth([p_v[k][z, at8, :] for z in range(CZ)])):
                zhl[z, at8, :] = plane
            return carry

        lax.fori_loop(0, B // R, depth, 0)
        for b in range(BLOCKS):
            hi, lo = split(zhl[:, ROWS * b : ROWS * b + ROWS, :].reshape(CZ * ROWS, B))
            t = dot(jnp.concatenate([hi, lo], axis=1), wy[...])
            hi, lo = split(t[:, :B] + t[:, B:])
            for z in range(CZ):
                half, rows = slice(128 * (z % 2), 128 * (z % 2) + 128), slice(ROWS * z, ROWS * z + ROWS)
                t2[z // 2, ROWS * b : ROWS * b + ROWS, half] = hi[rows]
                t2[z // 2, B + ROWS * b : B + ROWS * b + ROWS, half] = lo[rows]
        for i in range(CZ // 2):
            o = dot(wx[...], t2[i])
            o = o[:B] + o[B:]
            nl[2 * i] = o[:, :B]
            nl[2 * i + 1] = o[:, B:]

    def sweep(k, lo, hi):
        def body(i, carry):
            update(k, i)
            return carry

        lax.fori_loop(lo, hi, body, 0)

    def arrived(c):
        for copy in loads[4 * c : 4 * c + 4]:
            copy.wait()

    def sweep_all(k):
        if k == 0:
            arrived(0)
            arrived(1)
        sweep(k, 0, 1)
        if k == 0:
            enter()
        if k < OUTER - 1:
            start(faces(k))
        else:
            start(faces(k)[:2])
            sweep(k, 7, BLOCKS)
            start(ninth())
            start(faces(k)[2:])
            start(sides(k, 2))
        if k == 0:
            arrived(2)
        sweep(k, 1, 4)
        start(sides(k, 0))
        if k == 0:
            arrived(3)
            for copy in weights:
                copy.wait()
            start(statics())
        sweep(k, 4, 6)
        start(sides(k, 1))
        sweep(k, 6, 7)
        start(sides(k, 3))
        if k < OUTER - 1:
            sweep(k, 7, BLOCKS)
            start(sides(k, 2))

    def halos(k):
        finish(faces(k)[:2])
        hi, lo = split(xrec[k].reshape(2 * B, B))
        g = dot(jnp.concatenate([hi, lo], axis=1), wy[...])
        hi, lo = split(g[:, :B] + g[:, B:])
        o = dot(bx[...], jnp.concatenate([hi, lo], axis=1))
        o = o[: 2 * B, :B] + o[: 2 * B, B:] + o[2 * B :, :B]
        o = o.reshape(2, CZ, R, B)
        nl[:, 0:R, :] += o[0]
        nl[:, B - R :, :] += o[1]
        if k == OUTER - 1:
            finish(ninth())
            n_hi, n_lo = split(nine[...].reshape(B, B))
            n = dot(jnp.concatenate([n_hi, n_lo], axis=1), wy[...])
            n_hi, n_lo = split(n[:, :B] + n[:, B:])
            o = dot(
                bm[...],
                jnp.concatenate(
                    [jnp.concatenate([hi[:B], lo[:B]], axis=1), jnp.concatenate([n_hi, n_lo], axis=1)], axis=0
                ),
            )
            o = o[:B, :B] + o[:B, B:] + o[B:, :B]
            for z in range(CZ):
                half = slice(128 * (z % 2), 128 * (z % 2) + 128)
                own = t2[z // 2, 0:ROWS, half].astype(F32) + t2[z // 2, B : B + ROWS, half].astype(F32)
                own = jnp.sum(own[:R] * reach, axis=0, keepdims=True)
                nine[z] = o[R * z : R * z + R] + jnp.where(row8 == R - 1, own, 0.0)
        finish(faces(k)[2:])
        for c in range(4):
            finish(sides(k, c))
        hi, lo = split(jnp.concatenate([hrec[k, 0], hrec[k, 1]], axis=1))
        yh = dot(hi, by[0]) + dot(lo, by[0]) + dot(hi, by[1])
        hi, lo = split(yh)
        yhi[0 : B + 4 * R, :] = hi
        ylo[0 : B + 4 * R, :] = lo
        both = dot(ae[...], yhi[...])
        hout[...] = both[: B + R] + both[B + R :] + dot(ae[: B + R, :], ylo[...])

    for k in range(OUTER):
        sweep_all(k)
        own_part(k)
        halos(k)

    def stress(left, goal, p):
        return left * ((goal + SHIFT) * 0.5 - p)

    ends = [(rt, lf, rdma(OUTER, 0, fold, frec, 0, 1))]
    finish(statics())

    @pl.when(up)
    def _():
        for z in range(CZ):
            left = decay(nine[z] + halo_part(z, slice(B, B + R)), trow[z])
            here = stress(left, grow[z], xrec[OUTER - 1, 0, z])
            se[z, 0:R, :] = here
            turned = pltpu.roll(here, z + 1, 1)
            acc = turned if z == 0 else jnp.where(lane == z, turned, acc)
        fpack[0:R, :] = acc

    def last(i, carry):
        for at in rows_of(i):
            inside = pl.ds(pl.multiple_of(at.start + R, R), R)
            for z in range(CZ):
                left = damage_left(z, at)
                d_o[z, at, :] = 1.0 - left
                here = stress(left, g_v[z, at, :], p_o[z, at, :])
                se[z, inside, :] = here
                turned = pltpu.roll(here, z + 1, 1)
                acc = turned if z == 0 else jnp.where(lane == z, turned, acc)
            fpack[inside, :] = acc

        return carry

    lax.fori_loop(0, BLOCKS, last, 0)
    fold[0:R, :] = fpack[0:R, :]
    for h in range(2):
        acc = None
        for i in range(8):
            part = fpack[R * (8 * h + i + 1) : R * (8 * h + i + 2), :]
            acc = part if i == 0 else jnp.where(slot == i, pltpu.roll(part, 16 * i, 1), acc)
        fold[R * (h + 1) : R * (h + 2), :] = acc
    start(ends)

    def inner_forces(z, carry):
        prev = None
        for i in range(1, B // R + 1):
            at = slice(R * i, R * i + R)
            s = se[z, at, :]
            l = jnp.where(lane == 0, 0.0, pltpu.roll(s, 1, 1))
            total, other = l + s, l - s
            if prev is None:
                sum_up = jnp.where(row8 == 0, 0.0, pltpu.roll(total, 1, 0))
                dif_up = jnp.where(row8 == 0, 0.0, pltpu.roll(other, 1, 0))
            else:
                sum_up = pltpu.roll(jnp.where(row8 == R - 1, prev[0], total), 1, 0)
                dif_up = pltpu.roll(jnp.where(row8 == R - 1, prev[1], other), 1, 0)
            f_o[0, z, R * i - R : R * i, :] = 0.5 * (sum_up - total)
            f_o[1, z, R * i - R : R * i, :] = 0.5 * (dif_up + other)
            prev = total, other
        return carry

    lax.fori_loop(0, CZ, inner_forces, 0)
    finish(ends)


def forces(se, frec, p_v, d_v, f_i, p_h, d_h, f_h, f_v, sem):
    copies = [pltpu.make_async_copy(p_v, p_h, sem.at[0]), pltpu.make_async_copy(d_v, d_h, sem.at[1])]
    for copy in copies:
        copy.start()
    lane8 = lax.broadcasted_iota(jnp.int32, (R, B), 1)
    row8 = lax.broadcasted_iota(jnp.int32, (R, B), 0)
    first = lane8 == 0
    sides = []
    cols = [frec[0:R, :]]
    for i in range(B // R):
        col = frec[R * (i // 8 + 1) : R * (i // 8 + 2), :]
        cols.append(pltpu.roll(col, 128 - 16 * (i % 8), 1) if i % 8 else col)
    for i in range(1, B // R + 1):
        col, before = cols[i], cols[i - 1]
        up = pltpu.roll(jnp.where(row8 == R - 1, before, col), 1, 0)
        sides.append((0.5 * (up - col), 0.5 * (up + col)))
    for z in range(CZ):
        for i in range(B // R):
            at = slice(R * i, R * i + R)
            for c in range(2):
                part = sides[i][c]
                if z:
                    part = pltpu.roll(part, 128 - z, 1)
                f = f_i[c, z, at, :] + jnp.where(first, part, 0.0)
                if i == 0:
                    u = pltpu.roll(se[z, 0:R, :], 1, 0)
                    left = jnp.where(first, 0.0, pltpu.roll(u, 1, 1))
                    edge = 0.5 * (u + left) if c == 0 else 0.5 * (left - u)
                    f = f + jnp.where(row8 == 0, edge, 0.0)
                f_v[c, z, at, :] = f
        for c in range(2):
            copies.append(pltpu.make_async_copy(f_v.at[c, z], f_h.at[c, z], sem.at[2 + 2 * z + c]))
            copies[-1].start()
    for copy in copies:
        copy.wait()


def solution(mesh):
    nx, ny = mesh.shape["gx"], mesh.shape["gy"]
    consts = tables()
    hbm = pl.BlockSpec(memory_space=pltpu.MemorySpace.HBM)
    vmem = pl.BlockSpec(memory_space=pltpu.MemorySpace.VMEM)
    block = jax.ShapeDtypeStruct((CZ, B, B), F32)
    scratch = [
        pltpu.VMEM((CZ, B, B), F32),
        pltpu.VMEM((CZ, B, B), F32),
        pltpu.VMEM((CZ, B, B), jnp.int32),
        pltpu.VMEM((CZ, B, B), jnp.int32),
        pltpu.VMEM((CZ, B, B), F32),
        pltpu.VMEM((CZ, B, B), F32),
        pltpu.VMEM((OUTER - 1, CZ, B, B), F32),
        pltpu.VMEM((CZ, B, B), F32),
        pltpu.VMEM((CZ // 2, 2 * B, 2 * B), BF16),
        pltpu.VMEM((CZ, B, B), F32),
        pltpu.VMEM((B + R, 2 * B), F32),
        pltpu.VMEM((2 * B, 2 * B), BF16),
        pltpu.VMEM((2 * B, 2 * B), BF16),
        pltpu.VMEM((OUTER, 2, B, B), F32),
        pltpu.VMEM((OUTER, 2, B + 4 * R, B), F32),
        pltpu.VMEM((OUTER, 2, CZ, R, B), F32),
        pltpu.VMEM((2 * B, 2 * B), BF16),
        pltpu.VMEM((2 * B, 2 * B), BF16),
        pltpu.VMEM((2 * B + 2 * R, 2 * B), BF16),
        pltpu.VMEM((2, 2 * B, 2 * B), BF16),
        pltpu.VMEM((4 * B, 2 * B), BF16),
        pltpu.VMEM((2 * B, 2 * B), BF16),
        pltpu.VMEM((B + R, B), F32),
        pltpu.VMEM((3 * R, B), F32),
        pltpu.VMEM((CZ, R, B), F32),
        pltpu.VMEM((CZ, R, B), F32),
        pltpu.VMEM((CZ, R, B), F32),
        pltpu.SemaphoreType.DMA((4, 4)),
        pltpu.SemaphoreType.DMA((7,)),
        pltpu.SemaphoreType.DMA((OUTER + 1, 14)),
        pltpu.SemaphoreType.DMA((OUTER + 1, 14)),
    ]

    def local(*args):
        p, d, f, stress, column = pl.pallas_call(
            functools.partial(kernel, nx, ny),
            out_shape=(
                block,
                block,
                jax.ShapeDtypeStruct((2, CZ, B, B), F32),
                jax.ShapeDtypeStruct((CZ, B + R, B), F32),
                jax.ShapeDtypeStruct((3 * R, B), F32),
            ),
            in_specs=[hbm] * 11,
            out_specs=[vmem] * 5,
            scratch_shapes=scratch,
            compiler_params=pltpu.CompilerParams(
                collective_id=0, has_side_effects=True, vmem_limit_bytes=KERNEL_VMEM
            ),
        )(*[pltpu.with_memory_space_constraint(a, pltpu.MemorySpace.HBM) for a in (*args, *[jnp.asarray(c) for c in consts])])
        return pl.pallas_call(
            forces,
            out_shape=(block, block, jax.ShapeDtypeStruct((2, CZ, B, B), F32)),
            in_specs=[vmem] * 5,
            out_specs=[hbm] * 3,
            scratch_shapes=[pltpu.VMEM((2, CZ, B, B), F32), pltpu.SemaphoreType.DMA((2 + 2 * CZ,))],
            compiler_params=pltpu.CompilerParams(vmem_limit_bytes=FORCE_VMEM),
        )(stress, column, p, d, f)

    placed = P(None, "gx", "gy")
    return jax.shard_map(
        local,
        mesh=mesh,
        in_specs=(placed,) * 5,
        out_specs=(placed, placed, P(None, None, "gx", "gy")),
        check_vma=False,
    )
```
